32 devices in a mesh: tm: 2 (over y), pairs: 16 (over z, x, core).
Axes of the slice: x: 2, y: 2, z: 4, core: 2. Of those that a mesh axis runs over, the one named last changes fastest.
Arguments:
- records: bfloat16 [2, 512, 128, 2048], P('tm', 'pairs')
- source_map: int32 [2, 512], P('tm'), may hold values from 0 to 511, each once within a row
- pair_blocks: int32 [16, 6, 2], P('pairs'), may hold values from -1 to 31, as said below
Outputs:
- stacks: float32 [96, 16, 2, 128, 128], P('pairs', 'tm')
The draws below stay inside these ranges and needn't reach their ends.
Inputs may be any that keep to these rules, and one draw needn't show every extreme that they name: `pair_blocks`: each pair slot holds blocks i <= j with j - i <= 2, or -1 and -1 when empty; every such pair appears in exactly one slot; some owner has all 6 slots filled. `source_map`: each row is a permutation: every slot of a time group holds exactly one window of one channel block.
All inputs are finite; a program needn't handle non-finite values.
Results may differ from the reference program's by a relative error of at most 0.0056.
Values may be sent and summed in bfloat16 or wider, within the bound.
A program may use at most 128 MiB of HBM per device.

```python
import math
import jax
import jax.numpy as jnp
import numpy as np
from jax import lax

CB = 128
NB = 32
L = 2048
BINS = 16
FIRST_BIN = 64
DMAX = 2
WIN = 16
GROUP_ITEMS = 512
PC = 6
N_TM = 2
N_PAIRS = 16


def draw_records(key, part):
    first_key, second_key = jax.random.split(key, 2)
    shape_full = (N_TM, WIN * NB, CB, L)
    gains = jnp.exp(jax.random.uniform(second_key, (N_TM, WIN * NB, CB, 1), jnp.float32, 0.0, math.log(10.0)))
    base = jax.random.normal(first_key, shape_full, jnp.float32)
    return (base * gains).astype(jnp.bfloat16)


def draw_pair_blocks(key, part):
    listed = np.array([[start_block, start_block + offset] for offset in range(DMAX + 1) for start_block in range(NB - offset)], dtype=np.int32)
    total_slots = N_PAIRS * PC
    order = jax.random.permutation(jax.random.fold_in(key, 7), total_slots)[:listed.shape[0]]
    table_rows = jnp.full((total_slots, 2), -1, jnp.int32).at[order].set(jnp.asarray(listed))
    return table_rows.reshape(N_PAIRS, PC, 2)


def setup_inputs(seed: int = 0) -> dict:
    arg_keys = jax.random.split(jax.random.key(seed), 4)
    return {
        "records": draw_records(jax.random.fold_in(arg_keys[3], 71), 0),
        "source_map": jax.vmap(lambda own: jax.random.permutation(own, GROUP_ITEMS))(jax.random.split(arg_keys[1], N_TM)).reshape((N_TM, GROUP_ITEMS)).astype(jnp.int32),
        "pair_blocks": draw_pair_blocks(jax.random.fold_in(arg_keys[3], 71), 0),
    }


def transform_table(length):
    samples = jnp.arange(length, dtype=jnp.int32)
    bin_index = FIRST_BIN + jnp.arange(BINS, dtype=jnp.int32)
    phases = samples[:, None] * bin_index[None, :] % length
    angles = 2.0 * math.pi / length * phases.astype(jnp.float32)
    taper = 0.5 - 0.5 * jnp.cos(2.0 * math.pi / length * samples.astype(jnp.float32))
    weight_col = (taper / math.sqrt(length))[:, None]
    return jnp.concatenate([jnp.cos(angles) * weight_col, -jnp.sin(angles) * weight_col], axis=1).astype(jnp.bfloat16)

def whiten_spectra(windows, table):
    transformed = jnp.einsum('scn,nk->skc', windows.astype(jnp.float32), table.astype(jnp.float32), precision=lax.Precision.HIGHEST)
    real_part = transformed[:, :BINS]
    imag_part = transformed[:, BINS:]
    power = lax.optimization_barrier(jnp.mean(real_part * real_part + imag_part * imag_part, axis=2, keepdims=True))
    inverse = 1.0 / jnp.sqrt(power + 1e-06)
    return (transformed * jnp.concatenate([inverse, inverse], axis=1)).astype(jnp.bfloat16)

def reference(records, source_map, pair_blocks):
    table = transform_table(records.shape[3])
    spectra_all = lax.map(lambda group_rows: whiten_spectra(group_rows, table), records)
    ordered = jax.vmap(lambda spec_group, index_row: spec_group[index_row])(spectra_all, source_map)
    windows_total = ordered.shape[0] * WIN
    arranged = ordered.reshape(windows_total, NB, 2, BINS, ordered.shape[3])
    flat_pairs = pair_blocks.reshape(-1, 2)

    def one_pair(pair_row):
        valid = (pair_row[0] >= 0).astype(jnp.float32)
        safe_row = jnp.maximum(pair_row, 0).astype(jnp.int32)
        left_spec = arranged[:, safe_row[0]].astype(jnp.float32)
        right_spec = arranged[:, safe_row[1]].astype(jnp.float32)
        real_sum = jnp.einsum('wfi,wfj->fij', left_spec[:, 0], right_spec[:, 0]) + jnp.einsum('wfi,wfj->fij', left_spec[:, 1], right_spec[:, 1])
        imag_sum = jnp.einsum('wfi,wfj->fij', left_spec[:, 1], right_spec[:, 0]) - jnp.einsum('wfi,wfj->fij', left_spec[:, 0], right_spec[:, 1])
        return jnp.stack([real_sum, imag_sum], axis=1) * (valid / math.sqrt(windows_total))
    return lax.map(one_pair, flat_pairs)
```

```python
import functools
import math

import jax
import jax.numpy as jnp
import numpy as np
from jax import lax
from jax.experimental import pallas as pl
from jax.experimental.pallas import tpu as pltpu
from jax.sharding import PartitionSpec as P

NB = 32
BINS = 16
FIRST_BIN = 64
WIN = 16
MESH = pl.DeviceIdType.MESH


def transform_table(length):
    samples = np.arange(length)
    phases = samples[None, :] * (FIRST_BIN + np.arange(BINS))[:, None] % length
    angles = 2.0 * np.pi / length * phases
    weight = (0.5 - 0.5 * np.cos(2.0 * np.pi / length * samples)) / math.sqrt(length)
    rows = np.concatenate([np.cos(angles) * weight, -np.sin(angles) * weight])
    return rows.astype(np.float32).astype(jnp.bfloat16)


class Plan:
    def __init__(self, groups, pairs, items, channels):
        self.groups, self.pairs, self.items, self.channels = groups, pairs, items, channels
        self.depth = pairs // 4
        self.half = pairs // 2
        self.rows = min(8, items)
        self.pieces = items // self.rows
        self.bins = BINS // groups
        self.width = 2 * self.bins * channels
        middle = self.pieces // 2
        self.parts = [(k, 1) for k in range(middle)] + [(middle, self.pieces - middle)]
        self.doubled = (min(1, len(self.parts) - 1), groups - 1)


def gather_kernel(plan, blocks_hbm, map_hbm, table_hbm, records_ref, picked_ref,
                  stream, raw, own, spectra, maps, onehot, blocks_ref, table_ref,
                  load_sems, small_sems, recv_sems, twin_recv, z_send, side_send, twin_send,
                  tm_send, map_send, map_recv, keep_sems):
    groups, pairs, depth, half = plan.groups, plan.pairs, plan.depth, plan.half
    items, channels, length = records_ref.shape
    batch = stream.shape[1]
    depth_in = stream.shape[0]
    batches = items // batch
    per_piece = plan.rows // batch
    slots = blocks_ref.shape[2]
    t = lax.axis_index("tm")
    me = lax.axis_index("pairs")
    z = me // 4
    x = (me // 2) % 2
    c = me % 2
    place = x * depth + z
    up, down = me + 4, me - 4
    side = z * 4 + (1 - x) * 2 + c
    twin = z * 4 + x * 2 + 1 - c
    has_up = z < depth - 1
    has_down = z > 0

    def load(i):
        return pltpu.make_async_copy(
            records_ref.at[pl.ds(i * batch, batch)], stream.at[i % depth_in], load_sems.at[i % depth_in]
        )

    small = [
        pltpu.make_async_copy(table_hbm, table_ref, small_sems.at[0]),
        pltpu.make_async_copy(map_hbm, maps.at[t], small_sems.at[1]),
        pltpu.make_async_copy(blocks_hbm, blocks_ref, small_sems.at[2]),
    ]
    small[0].start()
    for i in range(min(depth_in, batches)):
        load(i).start()
    small[1].start()
    small[2].start()

    barrier = pltpu.get_barrier_semaphore()
    for d in range(1, groups):
        pl.semaphore_signal(barrier, inc=1, device_id=((t + d) % groups, me), device_id_type=MESH)
    for other in (side, twin):
        pl.semaphore_signal(barrier, inc=1, device_id=(t, other), device_id_type=MESH)

    @pl.when(has_up)
    def _():
        pl.semaphore_signal(barrier, inc=1, device_id=(t, up), device_id_type=MESH)

    @pl.when(has_down)
    def _():
        pl.semaphore_signal(barrier, inc=1, device_id=(t, down), device_id_type=MESH)

    def span(part):
        return pl.ds(*plan.parts[part])

    def landed(group, part, source):
        return spectra.at[group, span(part), c, source]

    def send(group, part, source, target, send_sem, recv_sem, kept):
        there = landed(group, part, source)
        return pltpu.make_async_remote_copy(
            src_ref=there if kept is None else kept,
            dst_ref=there,
            send_sem=send_sem,
            recv_sem=recv_sem,
            device_id=(t, target),
            device_id_type=MESH,
        )

    def to_twin(group, part, source, kept=None):
        send(group, part, source, twin, twin_send.at[0], twin_recv.at[group, part], kept).start()

    def spread(group, part, source, upward, downward, kept=None, across=True):
        recv = recv_sems.at[group, part, source]
        if upward is not None:
            @pl.when(upward)
            def _():
                send(group, part, source, up, z_send.at[0, source], recv, kept).start()
        if downward is not None:
            @pl.when(downward)
            def _():
                send(group, part, source, down, z_send.at[1, source], recv, kept).start()
        if across:
            send(group, part, source, side, side_send.at[group, part], recv, kept).start()
        to_twin(group, part, source, kept)

    def arrived(group, part, source):
        there = landed(group, part, source)
        pltpu.make_async_copy(there, there, recv_sems.at[group, part, source]).wait()

    def tm_copy(d, part):
        peer = (t + d) % groups
        return pltpu.make_async_remote_copy(
            src_ref=own.at[peer, span(part)],
            dst_ref=landed(t, part, place),
            send_sem=tm_send.at[d],
            recv_sem=recv_sems.at[t, part, place],
            device_id=(peer, me),
            device_id_type=MESH,
        )

    def map_copy(d):
        peer = (t + d) % groups
        return pltpu.make_async_remote_copy(
            src_ref=maps.at[t],
            dst_ref=maps.at[t],
            send_sem=map_send.at[d],
            recv_sem=map_recv.at[t],
            device_id=(peer, me),
            device_id_type=MESH,
        )

    def keep(k):
        return pltpu.make_async_copy(own.at[t, k], spectra.at[t, k, c, place], keep_sems.at[k])

    def from_tm(part):
        for d in range(1, groups):
            group = (t + d) % groups
            arrived(group, part, place)
            spread(group, part, place, has_up, has_down)

    def from_z(step, part, d, column=place, across=True):
        group = (t + d) % groups

        @pl.when(z - step >= 0)
        def _():
            arrived(group, part, column - step)
            spread(group, part, column - step, has_up, None, None, across)

        @pl.when(z + step < depth)
        def _():
            arrived(group, part, column + step)
            spread(group, part, column + step, None, has_down, None, across)

    other = (1 - x) * depth + z

    def from_side(step, part, d):
        group = (t + d) % groups

        @pl.when(z - step >= 0)
        def _():
            arrived(group, part, other - step)
            to_twin(group, part, other - step)

        @pl.when((step > 0) & (z + step < depth))
        def _():
            arrived(group, part, other + step)
            to_twin(group, part, other + step)

    def doubled_start():
        part, d = plan.doubled
        group = (t + d) % groups
        arrived(group, part, other)
        spread(group, part, other, has_up, has_down, None, False)

    def launch(parts):
        for part in parts:
            for d in range(1, groups):
                tm_copy(d, part).start()
        for part in parts:
            spread(t, part, place, has_up, has_down, own.at[t, span(part)])

    count = len(plan.parts)
    ready = {start + size - 1: part for part, (start, size) in enumerate(plan.parts)}
    steps = []
    for part in range(count):
        steps.append((from_tm, part))
        for d in range(1, groups):
            if part:
                steps.append((from_z, 1, part - 1, d))
        steps.append((from_z, 1, part, 0))
    steps += [(from_z, 1, count - 1, d) for d in range(1, groups)]
    early = 2 if plan.pieces >= 4 else 0

    def follow(some):
        for what, *which in some:
            if what is from_z:
                step, part, d = which
                from_z(step, part, d, place, (part, d) != plan.doubled)
                if (part, d) == plan.doubled:
                    doubled_start()
            else:
                what(*which)

    for k in range(plan.pieces):
        for j in range(per_piece):
            i = k * per_piece + j
            if i == 0:
                small[0].wait()
            load(i).wait()
            block = stream[i % depth_in].reshape(batch * channels, length)
            both = lax.dot_general(
                table_ref[...], block, (((1,), (1,)), ((), ())), preferred_element_type=jnp.float32
            )
            if i + depth_in < batches:
                load(i + depth_in).start()
            for r in range(batch):
                real = both[:BINS, r * channels:(r + 1) * channels]
                imag = both[BINS:, r * channels:(r + 1) * channels]
                power = jnp.mean(real * real + imag * imag, axis=1, keepdims=True)
                inverse = 1.0 / jnp.sqrt(power + 1e-06)
                raw[j * batch + r, :BINS] = real * inverse
                raw[j * batch + r, BINS:] = imag * inverse
        turned = jnp.transpose(raw[...], (1, 0, 2)).astype(jnp.bfloat16)
        for h in range(groups):
            for part in range(2):
                for f in range(plan.bins):
                    col = (part * plan.bins + f) * channels
                    own[h, k, :, col:col + channels] = turned[part * BINS + h * plan.bins + f]
        if k == 0:
            pl.semaphore_wait(
                barrier, groups + 1 + has_up.astype(jnp.int32) + has_down.astype(jnp.int32)
            )
        if k in ready:
            launch([ready[k]])
        keep(k).start()
        if k == 0:
            small[1].wait()
            for d in range(1, groups):
                map_copy(d).start()
            small[2].wait()
        if k == plan.pieces - 2:
            follow(steps[:early])
    follow(steps[early:])

    total = maps.shape[2]

    def choose(group):
        wanted = lax.broadcasted_iota(jnp.int32, (WIN, total), 0) * NB
        lane = lax.broadcasted_iota(jnp.int32, (WIN, total), 1)
        offset = lane - wanted
        table = jnp.broadcast_to(maps[group], (WIN, total))
        owner = table // items
        line = (owner % 2) * 2 + (owner // 2) % 2
        line = line * depth + owner // 4 + table % items // plan.rows * pairs
        line = line * plan.rows + table % plan.rows
        for ref in range(2 * slots):
            block = jnp.broadcast_to(
                blocks_ref[0, ref % 2:ref % 2 + 1, ref // 2:ref // 2 + 1], (WIN, 1)
            )
            found = jnp.sum(jnp.where(offset == block, line, 0), axis=1, keepdims=True)
            found = jnp.where(block >= 0, found, -1)
            hit = (lane == found).astype(jnp.float32).astype(jnp.bfloat16)
            onehot[group, ref * WIN:(ref + 1) * WIN, :] = hit

    choose(t)
    for d in range(1, groups):
        group = (t + d) % groups
        pltpu.make_async_copy(maps.at[group], maps.at[group], map_recv.at[group]).wait()
        choose(group)
    for k in range(plan.pieces):
        keep(k).wait()

    every = [(part, d) for part in range(count) for d in range(groups)]
    crossing = [e for e in every if e != plan.doubled]

    @pl.loop(2, depth)
    def _(step):
        for part, d in every:
            from_z(step, part, d, place, (part, d) != plan.doubled)
            if (part, d) == plan.doubled:
                from_z(step - 1, part, d, other, False)

    if depth > 1:
        from_z(depth - 1, *plan.doubled, other, False)

    @pl.loop(0, depth - 1)
    def _(step):
        for part, d in crossing:
            from_side(step, part, d)

    met = set()

    def pick(part, d):
        group = (t + d) % groups
        there = spectra.at[group, span(part), 1 - c]
        pltpu.make_async_copy(there, there, twin_recv.at[group, part]).wait()
        start, size = plan.parts[part]
        lines = slice(start * pairs * plan.rows, (start + size) * pairs * plan.rows)
        rows_in = spectra[group, start:start + size].reshape(size * pairs * plan.rows, plan.width)
        found = jnp.dot(onehot[group, :, lines], rows_in, preferred_element_type=jnp.float32)
        found = found.astype(jnp.bfloat16)
        picked_ref[group] = picked_ref[group] + found if d in met else found
        met.add(d)

    for index, e in enumerate(every):
        if e in crossing:
            from_side(depth - 1, *e)
        if index:
            pick(*every[index - 1])
    pick(*every[-1])

    for d in range(1, groups):
        map_copy(d).wait_send()
        sent = own.at[(t + d) % groups]
        pltpu.make_async_copy(sent, sent, tm_send.at[d]).wait()

    for zz in range(depth):
        for column in (x, 1 - x):
            if depth == 1:
                continue
            source = column * depth + zz
            sent = spectra.at[:, :, c, source]
            if column is not x:
                sent = landed((t + plan.doubled[1]) % groups, plan.doubled[0], source)

            @pl.when(has_up & (zz <= z))
            def _():
                pltpu.make_async_copy(sent, sent, z_send.at[0, source]).wait()

            @pl.when(has_down & (zz >= z))
            def _():
                pltpu.make_async_copy(sent, sent, z_send.at[1, source]).wait()

    for part, d in every:
        group = (t + d) % groups
        sent = spectra.at[group, span(part), c, pl.ds(x * depth, depth)]
        if (part, d) == plan.doubled:
            sent = landed(group, part, place)
        pltpu.make_async_copy(sent, sent, side_send.at[group, part]).wait()
    sent = spectra.at[:, :, c]
    pltpu.make_async_copy(sent, sent, twin_send.at[0]).wait()


def gather_picked(plan, pair_blocks, source_map, table, records):
    items, channels, length = records.shape
    slots = pair_blocks.shape[1]
    groups, pairs = plan.groups, plan.pairs
    batch = min(4, plan.rows)
    streams = 4
    total = source_map.shape[1]
    dtype = jnp.bfloat16
    hbm = pl.BlockSpec(memory_space=pltpu.HBM)
    return pl.pallas_call(
        functools.partial(gather_kernel, plan),
        out_shape=jax.ShapeDtypeStruct((groups, 2 * slots * WIN, plan.width), dtype),
        in_specs=[hbm, hbm, hbm, hbm],
        out_specs=pl.BlockSpec(memory_space=pltpu.VMEM),
        scratch_shapes=[
            pltpu.VMEM((streams, batch, channels, length), dtype),
            pltpu.VMEM((plan.rows, 2 * BINS, channels), jnp.float32),
            pltpu.VMEM((groups, plan.pieces, plan.rows, plan.width), dtype),
            pltpu.VMEM((groups, plan.pieces, 2, plan.half, plan.rows, plan.width), dtype),
            pltpu.VMEM((groups,) + source_map.shape, jnp.int32),
            pltpu.VMEM((groups, 2 * slots * WIN, total), dtype),
            pltpu.VMEM((1, 2, slots), jnp.int32),
            pltpu.VMEM(table.shape, dtype),
            pltpu.SemaphoreType.DMA((streams,)),
            pltpu.SemaphoreType.DMA((3,)),
            pltpu.SemaphoreType.DMA((groups, len(plan.parts), plan.half)),
            pltpu.SemaphoreType.DMA((groups, len(plan.parts))),
            pltpu.SemaphoreType.DMA((2, plan.half)),
            pltpu.SemaphoreType.DMA((groups, len(plan.parts))),
            pltpu.SemaphoreType.DMA((1,)),
            pltpu.SemaphoreType.DMA((groups,)),
            pltpu.SemaphoreType.DMA((groups,)),
            pltpu.SemaphoreType.DMA((groups,)),
            pltpu.SemaphoreType.DMA((plan.pieces,)),
        ],
        compiler_params=pltpu.CompilerParams(
            collective_id=0, has_side_effects=True, vmem_limit_bytes=48 << 20
        ),
        name="gather_picked",
    )(jnp.transpose(pair_blocks, (0, 2, 1)), source_map, table, records)


def stack_kernel(plan, scale, picked_ref, out_ref, done, sems):
    groups = plan.groups
    slots, bins, _, channels, _ = out_ref.shape

    def write(s, f):
        return pltpu.make_async_copy(done.at[s, f], out_ref.at[s, f], sems.at[s, f])

    for s in range(slots):
        left = slice(2 * s * WIN, (2 * s + 1) * WIN)
        right = slice((2 * s + 1) * WIN, (2 * s + 2) * WIN)
        for f in range(bins):
            real = slice(f * channels, (f + 1) * channels)
            imag = slice((bins + f) * channels, (bins + f + 1) * channels)
            x_re = [picked_ref[g, left, real] for g in range(groups)]
            x_im = [picked_ref[g, left, imag] for g in range(groups)]
            y_re = jnp.concatenate([picked_ref[g, right, real] for g in range(groups)], axis=0)
            y_im = jnp.concatenate([picked_ref[g, right, imag] for g in range(groups)], axis=0)
            lhs = jnp.concatenate(x_re + x_im, axis=0)
            rhs = jnp.concatenate(
                [
                    jnp.concatenate([y_re, -y_im], axis=1),
                    jnp.concatenate([y_im, y_re], axis=1),
                ],
                axis=0,
            )
            both = lax.dot_general(
                lhs, rhs, (((0,), (0,)), ((), ())), preferred_element_type=jnp.float32
            )
            done[s, f, 0] = both[:, :channels] * scale
            done[s, f, 1] = both[:, channels:] * scale
            write(s, f).start()
    for s in range(slots):
        for f in range(bins):
            write(s, f).wait()


def stack_pairs(plan, slots, picked):
    channels, bins = plan.channels, plan.bins
    scale = 1.0 / math.sqrt(WIN * plan.groups)
    vmem = pl.BlockSpec(memory_space=pltpu.VMEM)
    shape = (slots, bins, 2, channels, channels)
    return pl.pallas_call(
        functools.partial(stack_kernel, plan, scale),
        out_shape=jax.ShapeDtypeStruct(shape, jnp.float32),
        in_specs=[vmem],
        out_specs=pl.BlockSpec(memory_space=pl.ANY),
        scratch_shapes=[pltpu.VMEM(shape, jnp.float32), pltpu.SemaphoreType.DMA((slots, bins))],
        compiler_params=pltpu.CompilerParams(vmem_limit_bytes=40 << 20),
        name="stack_pairs",
    )(picked)


def per_device(groups, pairs, records, source_map, pair_blocks):
    table = jnp.asarray(transform_table(records.shape[3]))
    plan = Plan(groups, pairs, records.shape[1], records.shape[2])
    picked = gather_picked(plan, pair_blocks, source_map, table, records[0])
    return stack_pairs(plan, pair_blocks.shape[1], picked)


def solution(mesh):
    groups, pairs = mesh.shape["tm"], mesh.shape["pairs"]
    return jax.shard_map(
        functools.partial(per_device, groups, pairs),
        mesh=mesh,
        in_specs=(P("tm", "pairs", None, None), P("tm", None), P("pairs", None, None)),
        out_specs=P("pairs", "tm", None, None, None),
        check_vma=False,
    )
```

```python
import functools
import math

import jax
import jax.numpy as jnp
import numpy as np
from jax import lax
from jax.experimental import pallas as pl
from jax.experimental.pallas import tpu as pltpu
from jax.sharding import PartitionSpec as P

NB = 32
BINS = 16
FIRST_BIN = 64
WIN = 16
MESH = pl.DeviceIdType.MESH


def transform_table(length):
    samples = np.arange(length)
    phases = samples[None, :] * (FIRST_BIN + np.arange(BINS))[:, None] % length
    angles = 2.0 * np.pi / length * phases
    weight = (0.5 - 0.5 * np.cos(2.0 * np.pi / length * samples)) / math.sqrt(length)
    rows = np.concatenate([np.cos(angles) * weight, -np.sin(angles) * weight])
    return rows.astype(np.float32).astype(jnp.bfloat16)


class Plan:
    def __init__(self, groups, pairs, items, channels):
        self.groups, self.pairs, self.items, self.channels = groups, pairs, items, channels
        self.depth = pairs // 4
        self.half = pairs // 2
        self.rows = min(8, items)
        self.pieces = items // self.rows
        self.bins = BINS // groups
        self.width = 2 * self.bins * channels
        middle = self.pieces // 2
        self.parts = [(k, 1) for k in range(middle)] + [(middle, self.pieces - middle)]
        self.doubled = (min(1, len(self.parts) - 1), groups - 1)


def gather_kernel(plan, blocks_hbm, map_hbm, table_hbm, records_ref, picked_ref,
                  stream, raw, own, spectra, maps, onehot, blocks_ref, table_ref,
                  load_sems, small_sems, recv_sems, twin_recv, z_send, side_send, twin_send,
                  tm_send, map_send, map_recv, keep_sems):
    groups, pairs, depth, half = plan.groups, plan.pairs, plan.depth, plan.half
    items, channels, length = records_ref.shape
    batch = stream.shape[1]
    depth_in = stream.shape[0]
    batches = items // batch
    per_piece = plan.rows // batch
    slots = blocks_ref.shape[2]
    t = lax.axis_index("tm")
    me = lax.axis_index("pairs")
    z = me // 4
    x = (me // 2) % 2
    c = me % 2
    place = x * depth + z
    up, down = me + 4, me - 4
    side = z * 4 + (1 - x) * 2 + c
    twin = z * 4 + x * 2 + 1 - c
    has_up = z < depth - 1
    has_down = z > 0

    def load(i):
        return pltpu.make_async_copy(
            records_ref.at[pl.ds(i * batch, batch)], stream.at[i % depth_in], load_sems.at[i % depth_in]
        )

    small = [
        pltpu.make_async_copy(table_hbm, table_ref, small_sems.at[0]),
        pltpu.make_async_copy(map_hbm, maps.at[t], small_sems.at[1]),
        pltpu.make_async_copy(blocks_hbm, blocks_ref, small_sems.at[2]),
    ]
    small[0].start()
    ahead = depth_in - 1
    for i in range(min(ahead, batches)):
        load(i).start()
    small[1].start()
    small[2].start()

    barrier = pltpu.get_barrier_semaphore()
    for d in range(1, groups):
        pl.semaphore_signal(barrier, inc=1, device_id=((t + d) % groups, me), device_id_type=MESH)
    for other in (side, twin):
        pl.semaphore_signal(barrier, inc=1, device_id=(t, other), device_id_type=MESH)

    @pl.when(has_up)
    def _():
        pl.semaphore_signal(barrier, inc=1, device_id=(t, up), device_id_type=MESH)

    @pl.when(has_down)
    def _():
        pl.semaphore_signal(barrier, inc=1, device_id=(t, down), device_id_type=MESH)

    def span(part):
        return pl.ds(*plan.parts[part])

    def landed(group, part, source):
        return spectra.at[group, span(part), c, source]

    def send(group, part, source, target, send_sem, recv_sem, kept):
        there = landed(group, part, source)
        return pltpu.make_async_remote_copy(
            src_ref=there if kept is None else kept,
            dst_ref=there,
            send_sem=send_sem,
            recv_sem=recv_sem,
            device_id=(t, target),
            device_id_type=MESH,
        )

    def to_twin(group, part, source, kept=None):
        send(group, part, source, twin, twin_send.at[0], twin_recv.at[group, part], kept).start()

    def spread(group, part, source, upward, downward, kept=None, across=True):
        recv = recv_sems.at[group, part, source]
        if upward is not None:
            @pl.when(upward)
            def _():
                send(group, part, source, up, z_send.at[0, source], recv, kept).start()
        if downward is not None:
            @pl.when(downward)
            def _():
                send(group, part, source, down, z_send.at[1, source], recv, kept).start()
        if across:
            send(group, part, source, side, side_send.at[group, part], recv, kept).start()
        to_twin(group, part, source, kept)

    def arrived(group, part, source):
        there = landed(group, part, source)
        pltpu.make_async_copy(there, there, recv_sems.at[group, part, source]).wait()

    def tm_copy(d, part):
        peer = (t + d) % groups
        return pltpu.make_async_remote_copy(
            src_ref=own.at[peer, span(part)],
            dst_ref=landed(t, part, place),
            send_sem=tm_send.at[d],
            recv_sem=recv_sems.at[t, part, place],
            device_id=(peer, me),
            device_id_type=MESH,
        )

    def map_copy(d):
        peer = (t + d) % groups
        return pltpu.make_async_remote_copy(
            src_ref=maps.at[t],
            dst_ref=maps.at[t],
            send_sem=map_send.at[d],
            recv_sem=map_recv.at[t],
            device_id=(peer, me),
            device_id_type=MESH,
        )

    def keep(k):
        return pltpu.make_async_copy(own.at[t, k], spectra.at[t, k, c, place], keep_sems.at[k])

    def from_tm(part):
        for d in range(1, groups):
            group = (t + d) % groups
            arrived(group, part, place)
            spread(group, part, place, has_up, has_down)

    def from_z(step, part, d, column=place, across=True):
        group = (t + d) % groups

        @pl.when(z - step >= 0)
        def _():
            arrived(group, part, column - step)
            spread(group, part, column - step, has_up, None, None, across)

        @pl.when(z + step < depth)
        def _():
            arrived(group, part, column + step)
            spread(group, part, column + step, None, has_down, None, across)

    other = (1 - x) * depth + z

    def from_side(step, part, d):
        group = (t + d) % groups

        @pl.when(z - step >= 0)
        def _():
            arrived(group, part, other - step)
            to_twin(group, part, other - step)

        @pl.when((step > 0) & (z + step < depth))
        def _():
            arrived(group, part, other + step)
            to_twin(group, part, other + step)

    def doubled_start():
        part, d = plan.doubled
        group = (t + d) % groups
        arrived(group, part, other)
        spread(group, part, other, has_up, has_down, None, False)

    def launch(parts):
        for part in parts:
            for d in range(1, groups):
                tm_copy(d, part).start()
        for part in parts:
            spread(t, part, place, has_up, has_down, own.at[t, span(part)])

    total = maps.shape[2]

    def choose(group):
        wanted = lax.broadcasted_iota(jnp.int32, (WIN, total), 0) * NB
        lane = lax.broadcasted_iota(jnp.int32, (WIN, total), 1)
        offset = lane - wanted
        table = jnp.broadcast_to(maps[group], (WIN, total))
        owner = table // items
        line = (owner % 2) * 2 + (owner // 2) % 2
        line = line * depth + owner // 4 + table % items // plan.rows * pairs
        line = line * plan.rows + table % plan.rows
        for ref in range(2 * slots):
            block = jnp.broadcast_to(
                blocks_ref[0, ref % 2:ref % 2 + 1, ref // 2:ref // 2 + 1], (WIN, 1)
            )
            found = jnp.sum(jnp.where(offset == block, line, 0), axis=1, keepdims=True)
            found = jnp.where(block >= 0, found, -1)
            hit = (lane == found).astype(jnp.float32).astype(jnp.bfloat16)
            onehot[group, ref * WIN:(ref + 1) * WIN, :] = hit


    count = len(plan.parts)
    ready = {start + size - 1: part for part, (start, size) in enumerate(plan.parts)}
    steps = []
    for part in range(count):
        steps.append((from_tm, part))
        for d in range(1, groups):
            if part:
                steps.append((from_z, 1, part - 1, d))
        steps.append((from_z, 1, part, 0))
    steps += [(from_z, 1, count - 1, d) for d in range(1, groups)]
    early = 0
    hooks = {}
    if batches == 8 and count == 3:
        hooks = {4: [(from_tm, 0), (from_z, 1, 0, 0)], 6: [(from_tm, 1), (from_z, 1, 1, 0)]}
        steps = [(from_z, 1, 0, 1), (from_z, 1, 1, 1), (from_tm, 2), (from_z, 1, 2, 0), (from_z, 1, 2, 1)]

    def follow(some):
        for what, *which in some:
            if what is from_z:
                step, part, d = which
                from_z(step, part, d, place, (part, d) != plan.doubled)
                if (part, d) == plan.doubled:
                    doubled_start()
            else:
                what(*which)

    for k in range(plan.pieces):
        for j in range(per_piece):
            i = k * per_piece + j
            if i == 0:
                small[0].wait()
            load(i).wait()
            if i + ahead < batches:
                load(i + ahead).start()
            block = stream[i % depth_in].reshape(batch * channels, length)
            both = lax.dot_general(
                table_ref[...], block, (((1,), (1,)), ((), ())), preferred_element_type=jnp.float32
            )
            for r in range(batch):
                real = both[:BINS, r * channels:(r + 1) * channels]
                imag = both[BINS:, r * channels:(r + 1) * channels]
                power = jnp.mean(real * real + imag * imag, axis=1, keepdims=True)
                inverse = 1.0 / jnp.sqrt(power + 1e-06)
                raw[j * batch + r, :BINS] = real * inverse
                raw[j * batch + r, BINS:] = imag * inverse
            follow(hooks.get(i, []))
        turned = jnp.transpose(raw[...], (1, 0, 2)).astype(jnp.bfloat16)
        for h in range(groups):
            for part in range(2):
                for f in range(plan.bins):
                    col = (part * plan.bins + f) * channels
                    own[h, k, :, col:col + channels] = turned[part * BINS + h * plan.bins + f]
        if k == 0:
            pl.semaphore_wait(barrier, groups + 1 + has_up.astype(jnp.int32) + has_down.astype(jnp.int32))
            small[1].wait()
            for d in range(1, groups):
                map_copy(d).start()
        if k in ready:
            launch([ready[k]])
        keep(k).start()
        if k == plan.pieces - 2:
            follow(steps[:early])
    follow(steps[early:])
    small[2].wait()
    choose(t)

    for d in range(1, groups):
        group = (t + d) % groups
        pltpu.make_async_copy(maps.at[group], maps.at[group], map_recv.at[group]).wait()
        choose(group)
    for k in range(plan.pieces):
        keep(k).wait()

    every = [(part, d) for part in range(count) for d in range(groups)]
    crossing = [e for e in every if e != plan.doubled]

    @pl.loop(2, depth)
    def _(step):
        for part, d in every:
            from_z(step, part, d, place, (part, d) != plan.doubled)
            if (part, d) == plan.doubled:
                from_z(step - 1, part, d, other, False)

    if depth > 1:
        from_z(depth - 1, *plan.doubled, other, False)

    @pl.loop(0, depth - 2)
    def _(step):
        for part, d in crossing:
            from_side(step, part, d)

    def pick(d):
        group = (t + d) % groups
        for part in range(count):
            there = spectra.at[group, span(part), 1 - c]
            pltpu.make_async_copy(there, there, twin_recv.at[group, part]).wait()
        rows_in = spectra[group].reshape(total, plan.width)
        found = jnp.dot(onehot[group], rows_in, preferred_element_type=jnp.float32)
        picked_ref[group] = found.astype(jnp.bfloat16)

    for part, d in every:
        if (part, d) in crossing:
            if depth > 1:
                from_side(depth - 2, part, d)
            from_side(depth - 1, part, d)
        if part == count - 1:
            if d:
                pick(d - 1)
    pick(groups - 1)

    for d in range(1, groups):
        map_copy(d).wait_send()
        sent = own.at[(t + d) % groups]
        pltpu.make_async_copy(sent, sent, tm_send.at[d]).wait()

    for zz in range(depth):
        for column in (x, 1 - x):
            if depth == 1:
                continue
            source = column * depth + zz
            sent = spectra.at[:, :, c, source]
            if column is not x:
                sent = landed((t + plan.doubled[1]) % groups, plan.doubled[0], source)

            @pl.when(has_up & (zz <= z))
            def _():
                pltpu.make_async_copy(sent, sent, z_send.at[0, source]).wait()

            @pl.when(has_down & (zz >= z))
            def _():
                pltpu.make_async_copy(sent, sent, z_send.at[1, source]).wait()

    for part, d in every:
        group = (t + d) % groups
        sent = spectra.at[group, span(part), c, pl.ds(x * depth, depth)]
        if (part, d) == plan.doubled:
            sent = landed(group, part, place)
        pltpu.make_async_copy(sent, sent, side_send.at[group, part]).wait()
    sent = spectra.at[:, :, c]
    pltpu.make_async_copy(sent, sent, twin_send.at[0]).wait()


def gather_picked(plan, pair_blocks, source_map, table, records):
    items, channels, length = records.shape
    slots = pair_blocks.shape[1]
    groups, pairs = plan.groups, plan.pairs
    batch = min(4, plan.rows)
    streams = 3
    total = source_map.shape[1]
    dtype = jnp.bfloat16
    hbm = pl.BlockSpec(memory_space=pltpu.HBM)
    return pl.pallas_call(
        functools.partial(gather_kernel, plan),
        out_shape=jax.ShapeDtypeStruct((groups, 2 * slots * WIN, plan.width), dtype),
        in_specs=[hbm, hbm, hbm, hbm],
        out_specs=pl.BlockSpec(memory_space=pltpu.VMEM),
        scratch_shapes=[
            pltpu.VMEM((streams, batch, channels, length), dtype),
            pltpu.VMEM((plan.rows, 2 * BINS, channels), jnp.float32),
            pltpu.VMEM((groups, plan.pieces, plan.rows, plan.width), dtype),
            pltpu.VMEM((groups, plan.pieces, 2, plan.half, plan.rows, plan.width), dtype),
            pltpu.VMEM((groups,) + source_map.shape, jnp.int32),
            pltpu.VMEM((groups, 2 * slots * WIN, total), dtype),
            pltpu.VMEM((1, 2, slots), jnp.int32),
            pltpu.VMEM(table.shape, dtype),
            pltpu.SemaphoreType.DMA((streams,)),
            pltpu.SemaphoreType.DMA((3,)),
            pltpu.SemaphoreType.DMA((groups, len(plan.parts), plan.half)),
            pltpu.SemaphoreType.DMA((groups, len(plan.parts))),
            pltpu.SemaphoreType.DMA((2, plan.half)),
            pltpu.SemaphoreType.DMA((groups, len(plan.parts))),
            pltpu.SemaphoreType.DMA((1,)),
            pltpu.SemaphoreType.DMA((groups,)),
            pltpu.SemaphoreType.DMA((groups,)),
            pltpu.SemaphoreType.DMA((groups,)),
            pltpu.SemaphoreType.DMA((plan.pieces,)),
        ],
        compiler_params=pltpu.CompilerParams(
            collective_id=0, has_side_effects=True, vmem_limit_bytes=48 << 20
        ),
        name="gather_picked",
    )(
        pltpu.with_memory_space_constraint(jnp.transpose(pair_blocks, (0, 2, 1)), pltpu.HBM),
        pltpu.with_memory_space_constraint(source_map, pltpu.HBM),
        pltpu.with_memory_space_constraint(table, pltpu.HBM),
        records,
    )


def stack_kernel(plan, scale, picked_ref, out_ref, done, sems):
    groups = plan.groups
    slots, bins, _, channels, _ = out_ref.shape

    def write(s, f):
        return pltpu.make_async_copy(done.at[s, f], out_ref.at[s, f], sems.at[s, f])

    for s in range(slots):
        left = slice(2 * s * WIN, (2 * s + 1) * WIN)
        right = slice((2 * s + 1) * WIN, (2 * s + 2) * WIN)
        for f in range(bins):
            real = slice(f * channels, (f + 1) * channels)
            imag = slice((bins + f) * channels, (bins + f + 1) * channels)
            x_re = [picked_ref[g, left, real] for g in range(groups)]
            x_im = [picked_ref[g, left, imag] for g in range(groups)]
            y_re = jnp.concatenate([picked_ref[g, right, real] for g in range(groups)], axis=0)
            y_im = jnp.concatenate([picked_ref[g, right, imag] for g in range(groups)], axis=0)
            lhs = jnp.concatenate(x_re + x_im, axis=0)
            rhs = jnp.concatenate(
                [
                    jnp.concatenate([y_re, -y_im], axis=1),
                    jnp.concatenate([y_im, y_re], axis=1),
                ],
                axis=0,
            )
            both = lax.dot_general(
                lhs, rhs, (((0,), (0,)), ((), ())), preferred_element_type=jnp.float32
            )
            done[s, f, 0] = both[:, :channels] * scale
            done[s, f, 1] = both[:, channels:] * scale
            write(s, f).start()
    for s in range(slots):
        for f in range(bins):
            write(s, f).wait()


def stack_pairs(plan, slots, picked):
    channels, bins = plan.channels, plan.bins
    scale = 1.0 / math.sqrt(WIN * plan.groups)
    vmem = pl.BlockSpec(memory_space=pltpu.VMEM)
    shape = (slots, bins, 2, channels, channels)
    return pl.pallas_call(
        functools.partial(stack_kernel, plan, scale),
        out_shape=jax.ShapeDtypeStruct(shape, jnp.float32),
        in_specs=[vmem],
        out_specs=pl.BlockSpec(memory_space=pl.ANY),
        scratch_shapes=[pltpu.VMEM(shape, jnp.float32), pltpu.SemaphoreType.DMA((slots, bins))],
        compiler_params=pltpu.CompilerParams(vmem_limit_bytes=40 << 20),
        name="stack_pairs",
    )(picked)


def per_device(groups, pairs, records, source_map, pair_blocks):
    table = jnp.asarray(transform_table(records.shape[3]))
    plan = Plan(groups, pairs, records.shape[1], records.shape[2])
    picked = gather_picked(plan, pair_blocks, source_map, table, records[0])
    return stack_pairs(plan, pair_blocks.shape[1], picked)


def solution(mesh):
    groups, pairs = mesh.shape["tm"], mesh.shape["pairs"]
    return jax.shard_map(
        functools.partial(per_device, groups, pairs),
        mesh=mesh,
        in_specs=(P("tm", "pairs", None, None), P("tm", None), P("pairs", None, None)),
        out_specs=P("pairs", "tm", None, None, None),
        check_vma=False,
    )
```

```python
import functools
import math

import jax
import jax.numpy as jnp
import numpy as np
from jax import lax
from jax.experimental import pallas as pl
from jax.experimental.pallas import tpu as pltpu
from jax.sharding import PartitionSpec as P

NB = 32
BINS = 16
FIRST_BIN = 64
WIN = 16
MESH = pl.DeviceIdType.MESH


def transform_table(length):
    samples = np.arange(length)
    phases = samples[None, :] * (FIRST_BIN + np.arange(BINS))[:, None] % length
    angles = 2.0 * np.pi / length * phases
    weight = (0.5 - 0.5 * np.cos(2.0 * np.pi / length * samples)) / math.sqrt(length)
    rows = np.concatenate([np.cos(angles) * weight, -np.sin(angles) * weight])
    return rows.astype(np.float32).astype(jnp.bfloat16)


class Plan:
    def __init__(self, groups, pairs, items, channels):
        self.groups, self.pairs, self.items, self.channels = groups, pairs, items, channels
        self.depth = pairs // 4
        self.half = pairs // 2
        self.rows = min(8, items)
        self.pieces = items // self.rows
        self.bins = BINS // groups
        self.width = 2 * self.bins * channels
        middle = self.pieces // 2
        self.parts = [(k, 1) for k in range(self.pieces)]
        self.doubled = (min(3, len(self.parts) - 1), 0)


def gather_kernel(plan, blocks_hbm, map_hbm, table_hbm, records_ref, picked_ref,
                  stream, raw, own, spectra, maps, onehot, blocks_ref, table_ref,
                  load_sems, small_sems, recv_sems, twin_recv, z_send, side_send, twin_send,
                  tm_send, map_send, map_recv, keep_sems):
    groups, pairs, depth, half = plan.groups, plan.pairs, plan.depth, plan.half
    items, channels, length = records_ref.shape
    batch = stream.shape[1]
    depth_in = stream.shape[0]
    batches = items // batch
    per_piece = plan.rows // batch
    slots = blocks_ref.shape[2]
    t = lax.axis_index("tm")
    me = lax.axis_index("pairs")
    z = me // 4
    x = (me // 2) % 2
    c = me % 2
    place = x * depth + z
    up, down = me + 4, me - 4
    side = z * 4 + (1 - x) * 2 + c
    twin = z * 4 + x * 2 + 1 - c
    has_up = z < depth - 1
    has_down = z > 0
    out = 2 * (z // (depth // 2)) - 1

    def load(i):
        return pltpu.make_async_copy(
            records_ref.at[pl.ds(i * batch, batch)], stream.at[i % depth_in], load_sems.at[i % depth_in]
        )

    small = [
        pltpu.make_async_copy(table_hbm, table_ref, small_sems.at[0]),
        pltpu.make_async_copy(map_hbm, maps.at[t], small_sems.at[1]),
        pltpu.make_async_copy(blocks_hbm, blocks_ref, small_sems.at[2]),
    ]
    small[0].start()
    ahead = depth_in - 1
    for i in range(min(ahead, batches)):
        load(i).start()
    small[1].start()
    small[2].start()

    barrier = pltpu.get_barrier_semaphore()
    for d in range(1, groups):
        pl.semaphore_signal(barrier, inc=1, device_id=((t + d) % groups, me), device_id_type=MESH)
    for other in (side, twin):
        pl.semaphore_signal(barrier, inc=1, device_id=(t, other), device_id_type=MESH)

    @pl.when(has_up)
    def _():
        pl.semaphore_signal(barrier, inc=1, device_id=(t, up), device_id_type=MESH)

    @pl.when(has_down)
    def _():
        pl.semaphore_signal(barrier, inc=1, device_id=(t, down), device_id_type=MESH)

    def span(part):
        return pl.ds(*plan.parts[part])

    def landed(group, part, source):
        return spectra.at[group, span(part), c, source]

    def send(group, part, source, target, send_sem, recv_sem, kept):
        there = landed(group, part, source)
        return pltpu.make_async_remote_copy(
            src_ref=there if kept is None else kept,
            dst_ref=there,
            send_sem=send_sem,
            recv_sem=recv_sem,
            device_id=(t, target),
            device_id_type=MESH,
        )

    def to_twin(group, part, source, kept=None):
        send(group, part, source, twin, twin_send.at[0], twin_recv.at[group, part], kept).start()

    def spread(group, part, source, upward, downward, kept=None, across=True):
        recv = recv_sems.at[group, part, source]
        if upward is not None:
            @pl.when(upward)
            def _():
                send(group, part, source, up, z_send.at[0, source], recv, kept).start()
        if downward is not None:
            @pl.when(downward)
            def _():
                send(group, part, source, down, z_send.at[1, source], recv, kept).start()
        if across:
            send(group, part, source, side, side_send.at[group, part], recv, kept).start()
        to_twin(group, part, source, kept)

    def arrived(group, part, source):
        there = landed(group, part, source)
        pltpu.make_async_copy(there, there, recv_sems.at[group, part, source]).wait()

    def tm_copy(d, part):
        peer = (t + d) % groups
        return pltpu.make_async_remote_copy(
            src_ref=own.at[peer, span(part)],
            dst_ref=landed(t, part, place),
            send_sem=tm_send.at[d],
            recv_sem=recv_sems.at[t, part, place],
            device_id=(peer, me),
            device_id_type=MESH,
        )

    def map_copy(d):
        peer = (t + d) % groups
        return pltpu.make_async_remote_copy(
            src_ref=maps.at[t],
            dst_ref=maps.at[t],
            send_sem=map_send.at[d],
            recv_sem=map_recv.at[t],
            device_id=(peer, me),
            device_id_type=MESH,
        )

    def keep(k):
        return pltpu.make_async_copy(own.at[t, k], spectra.at[t, k, c, place], keep_sems.at[k])

    def from_tm(part):
        for d in range(1, groups):
            group = (t + d) % groups
            arrived(group, part, place)
            spread(group, part, place, has_up, has_down)

    def passed(toward, step, part, d, column, across):
        group = (t + d) % groups
        source = z + toward * step

        @pl.when((source >= 0) & (source < depth))
        def _():
            come = column + toward * step
            arrived(group, part, come)
            onward = z - toward

            @pl.when((onward >= 0) & (onward < depth))
            def _():
                send(group, part, come, me - 4 * toward, z_send.at[(1 + toward) // 2, come],
                     recv_sems.at[group, part, come], None).start()

            spread(group, part, come, None, None, None, across)

    def from_out(step, part, d, column=place, across=True):
        passed(out, step, part, d, column, across and (part, d) != plan.doubled)

    def from_in(step, part, d, column=place, across=True):
        passed(-out, step, part, d, column, across and (part, d) != plan.doubled)

    other = (1 - x) * depth + z

    def from_side(step, part, d):
        group = (t + d) % groups

        @pl.when(z - step >= 0)
        def _():
            arrived(group, part, other - step)
            to_twin(group, part, other - step)

        @pl.when((step > 0) & (z + step < depth))
        def _():
            arrived(group, part, other + step)
            to_twin(group, part, other + step)

    def doubled_start():
        part, d = plan.doubled
        group = (t + d) % groups
        arrived(group, part, other)
        spread(group, part, other, has_up, has_down, None, False)

    def launch(parts):
        for part in parts:
            for d in range(1, groups):
                tm_copy(d, part).start()
        for part in parts:
            spread(t, part, place, has_up, has_down, own.at[t, span(part)])

    total = maps.shape[2]

    def choose(group):
        wanted = lax.broadcasted_iota(jnp.int32, (WIN, total), 0) * NB
        lane = lax.broadcasted_iota(jnp.int32, (WIN, total), 1)
        offset = lane - wanted
        table = jnp.broadcast_to(maps[group], (WIN, total))
        owner = table // items
        line = (owner % 2) * 2 + (owner // 2) % 2
        line = line * depth + owner // 4 + table % items // plan.rows * pairs
        line = line * plan.rows + table % plan.rows
        for ref in range(2 * slots):
            block = jnp.broadcast_to(
                blocks_ref[0, ref % 2:ref % 2 + 1, ref // 2:ref // 2 + 1], (WIN, 1)
            )
            found = jnp.sum(jnp.where(offset == block, line, 0), axis=1, keepdims=True)
            found = jnp.where(block >= 0, found, -1)
            hit = (lane == found).astype(jnp.float32).astype(jnp.bfloat16)
            onehot[group, ref * WIN:(ref + 1) * WIN, :] = hit


    count = len(plan.parts)
    ready = {start + size - 1: part for part, (start, size) in enumerate(plan.parts)}
    far = range(1, groups)
    hooks = {}
    if batches == 8 and count == 4:
        hooks = {
            4: [(from_tm, 0), (from_out, 1, 0, 0)],
            5: [(from_in, 1, 0, 0)],
            6: [(from_tm, 1), (from_out, 1, 1, 0)],
        }
        steps = [(from_in, 1, 1, 0), (from_tm, 2)]
        steps += [(what, 1, part, d) for what in (from_out, from_in) for part in (0, 1) for d in far]
        steps += [(from_tm, 3), (doubled_start,)]
        steps += [(what, 1, part, d) for part in (2, 3) for what in (from_out, from_in) for d in range(groups)]
    else:
        steps = [(from_tm, part) for part in range(count)] + [(doubled_start,)]
        for what in (from_out, from_in):
            steps += [(what, 1, part, d) for part in range(count) for d in range(groups)]

    def follow(some):
        for what, *which in some:
            what(*which)

    for k in range(plan.pieces):
        for j in range(per_piece):
            i = k * per_piece + j
            if i == 0:
                small[0].wait()
            load(i).wait()
            if i + ahead < batches:
                load(i + ahead).start()
            block = stream[i % depth_in].reshape(batch * channels, length)
            both = lax.dot_general(
                table_ref[...], block, (((1,), (1,)), ((), ())), preferred_element_type=jnp.float32
            )
            for r in range(batch):
                real = both[:BINS, r * channels:(r + 1) * channels]
                imag = both[BINS:, r * channels:(r + 1) * channels]
                power = jnp.mean(real * real + imag * imag, axis=1, keepdims=True)
                inverse = 1.0 / jnp.sqrt(power + 1e-06)
                raw[j * batch + r, :BINS] = real * inverse
                raw[j * batch + r, BINS:] = imag * inverse
            follow(hooks.get(i, []))
        turned = jnp.transpose(raw[...], (1, 0, 2)).astype(jnp.bfloat16)
        for h in range(groups):
            for part in range(2):
                for f in range(plan.bins):
                    col = (part * plan.bins + f) * channels
                    own[h, k, :, col:col + channels] = turned[part * BINS + h * plan.bins + f]
        if k == 0:
            pl.semaphore_wait(barrier, groups + 1 + has_up.astype(jnp.int32) + has_down.astype(jnp.int32))
            small[1].wait()
            for d in range(1, groups):
                map_copy(d).start()
        if k in ready:
            launch([ready[k]])
        keep(k).start()
    follow(steps)
    for k in range(plan.pieces):
        keep(k).wait()

    every = [(part, d) for part in range(count) for d in range(groups)]
    crossing = [e for e in every if e != plan.doubled]

    @pl.loop(2, depth)
    def _(step):
        for what in (from_out, from_in):
            for part, d in every:
                what(step, part, d)
                if (part, d) == plan.doubled:
                    what(step - 1, part, d, other, False)
        for part, d in crossing:
            from_side(step - 2, part, d)

    for what in (from_out, from_in):
        what(depth - 1, *plan.doubled, other, False)

    small[2].wait()
    choose(t)

    for d in range(1, groups):
        group = (t + d) % groups
        pltpu.make_async_copy(maps.at[group], maps.at[group], map_recv.at[group]).wait()
        choose(group)
    def pick(d):
        group = (t + d) % groups
        for part in range(count):
            there = spectra.at[group, span(part), 1 - c]
            pltpu.make_async_copy(there, there, twin_recv.at[group, part]).wait()
        rows_in = spectra[group].reshape(total, plan.width)
        found = jnp.dot(onehot[group], rows_in, preferred_element_type=jnp.float32)
        picked_ref[group] = found.astype(jnp.bfloat16)

    for part, d in every:
        if (part, d) in crossing:
            if depth > 1:
                from_side(depth - 2, part, d)
            from_side(depth - 1, part, d)
        if part == count - 1:
            if d:
                pick(d - 1)
    pick(groups - 1)

    for d in range(1, groups):
        map_copy(d).wait_send()
        sent = own.at[(t + d) % groups]
        pltpu.make_async_copy(sent, sent, tm_send.at[d]).wait()

    for zz in range(depth):
        for column in (x, 1 - x):
            if depth == 1:
                continue
            source = column * depth + zz
            sent = spectra.at[:, :, c, source]
            if column is not x:
                sent = landed((t + plan.doubled[1]) % groups, plan.doubled[0], source)

            @pl.when(has_up & (zz <= z))
            def _():
                pltpu.make_async_copy(sent, sent, z_send.at[0, source]).wait()

            @pl.when(has_down & (zz >= z))
            def _():
                pltpu.make_async_copy(sent, sent, z_send.at[1, source]).wait()

    for part, d in every:
        group = (t + d) % groups
        sent = spectra.at[group, span(part), c, pl.ds(x * depth, depth)]
        if (part, d) == plan.doubled:
            sent = landed(group, part, place)
        pltpu.make_async_copy(sent, sent, side_send.at[group, part]).wait()
    sent = spectra.at[:, :, c]
    pltpu.make_async_copy(sent, sent, twin_send.at[0]).wait()


def gather_picked(plan, pair_blocks, source_map, table, records):
    items, channels, length = records.shape
    slots = pair_blocks.shape[1]
    groups, pairs = plan.groups, plan.pairs
    batch = min(4, plan.rows)
    streams = 3
    total = source_map.shape[1]
    dtype = jnp.bfloat16
    hbm = pl.BlockSpec(memory_space=pltpu.HBM)
    return pl.pallas_call(
        functools.partial(gather_kernel, plan),
        out_shape=jax.ShapeDtypeStruct((groups, 2 * slots * WIN, plan.width), dtype),
        in_specs=[hbm, hbm, hbm, hbm],
        out_specs=pl.BlockSpec(memory_space=pltpu.VMEM),
        scratch_shapes=[
            pltpu.VMEM((streams, batch, channels, length), dtype),
            pltpu.VMEM((plan.rows, 2 * BINS, channels), jnp.float32),
            pltpu.VMEM((groups, plan.pieces, plan.rows, plan.width), dtype),
            pltpu.VMEM((groups, plan.pieces, 2, plan.half, plan.rows, plan.width), dtype),
            pltpu.VMEM((groups,) + source_map.shape, jnp.int32),
            pltpu.VMEM((groups, 2 * slots * WIN, total), dtype),
            pltpu.VMEM((1, 2, slots), jnp.int32),
            pltpu.VMEM(table.shape, dtype),
            pltpu.SemaphoreType.DMA((streams,)),
            pltpu.SemaphoreType.DMA((3,)),
            pltpu.SemaphoreType.DMA((groups, len(plan.parts), plan.half)),
            pltpu.SemaphoreType.DMA((groups, len(plan.parts))),
            pltpu.SemaphoreType.DMA((2, plan.half)),
            pltpu.SemaphoreType.DMA((groups, len(plan.parts))),
            pltpu.SemaphoreType.DMA((1,)),
            pltpu.SemaphoreType.DMA((groups,)),
            pltpu.SemaphoreType.DMA((groups,)),
            pltpu.SemaphoreType.DMA((groups,)),
            pltpu.SemaphoreType.DMA((plan.pieces,)),
        ],
        compiler_params=pltpu.CompilerParams(
            collective_id=0, has_side_effects=True, vmem_limit_bytes=48 << 20
        ),
        name="gather_picked",
    )(
        pltpu.with_memory_space_constraint(jnp.transpose(pair_blocks, (0, 2, 1)), pltpu.HBM),
        pltpu.with_memory_space_constraint(source_map, pltpu.HBM),
        pltpu.with_memory_space_constraint(table, pltpu.HBM),
        records,
    )


def stack_kernel(plan, scale, picked_ref, out_ref, done, sems):
    groups = plan.groups
    slots, bins, _, channels, _ = out_ref.shape

    def write(s, f):
        return pltpu.make_async_copy(done.at[s, f], out_ref.at[s, f], sems.at[s, f])

    for s in range(slots):
        left = slice(2 * s * WIN, (2 * s + 1) * WIN)
        right = slice((2 * s + 1) * WIN, (2 * s + 2) * WIN)
        for f in range(bins):
            real = slice(f * channels, (f + 1) * channels)
            imag = slice((bins + f) * channels, (bins + f + 1) * channels)
            x_re = [picked_ref[g, left, real] for g in range(groups)]
            x_im = [picked_ref[g, left, imag] for g in range(groups)]
            y_re = jnp.concatenate([picked_ref[g, right, real] for g in range(groups)], axis=0)
            y_im = jnp.concatenate([picked_ref[g, right, imag] for g in range(groups)], axis=0)
            lhs = jnp.concatenate(x_re + x_im, axis=0)
            rhs = jnp.concatenate(
                [
                    jnp.concatenate([y_re, -y_im], axis=1),
                    jnp.concatenate([y_im, y_re], axis=1),
                ],
                axis=0,
            )
            both = lax.dot_general(
                lhs, rhs, (((0,), (0,)), ((), ())), preferred_element_type=jnp.float32
            )
            done[s, f, 0] = both[:, :channels] * scale
            done[s, f, 1] = both[:, channels:] * scale
            write(s, f).start()
    for s in range(slots):
        for f in range(bins):
            write(s, f).wait()


def stack_pairs(plan, slots, picked):
    channels, bins = plan.channels, plan.bins
    scale = 1.0 / math.sqrt(WIN * plan.groups)
    vmem = pl.BlockSpec(memory_space=pltpu.VMEM)
    shape = (slots, bins, 2, channels, channels)
    return pl.pallas_call(
        functools.partial(stack_kernel, plan, scale),
        out_shape=jax.ShapeDtypeStruct(shape, jnp.float32),
        in_specs=[vmem],
        out_specs=pl.BlockSpec(memory_space=pl.ANY),
        scratch_shapes=[pltpu.VMEM(shape, jnp.float32), pltpu.SemaphoreType.DMA((slots, bins))],
        compiler_params=pltpu.CompilerParams(vmem_limit_bytes=40 << 20),
        name="stack_pairs",
    )(picked)


def per_device(groups, pairs, records, source_map, pair_blocks):
    table = jnp.asarray(transform_table(records.shape[3]))
    plan = Plan(groups, pairs, records.shape[1], records.shape[2])
    picked = gather_picked(plan, pair_blocks, source_map, table, records[0])
    return stack_pairs(plan, pair_blocks.shape[1], picked)


def solution(mesh):
    groups, pairs = mesh.shape["tm"], mesh.shape["pairs"]
    return jax.shard_map(
        functools.partial(per_device, groups, pairs),
        mesh=mesh,
        in_specs=(P("tm", "pairs", None, None), P("tm", None), P("pairs", None, None)),
        out_specs=P("pairs", "tm", None, None, None),
        check_vma=False,
    )
```

```python
import functools
import math

import jax
import jax.numpy as jnp
import numpy as np
from jax import lax
from jax.experimental import pallas as pl
from jax.experimental.pallas import tpu as pltpu
from jax.sharding import PartitionSpec as P

NB = 32
BINS = 16
FIRST_BIN = 64
WIN = 16
MESH = pl.DeviceIdType.MESH


def transform_table(length):
    samples = np.arange(length)
    phases = samples[None, :] * (FIRST_BIN + np.arange(BINS))[:, None] % length
    angles = 2.0 * np.pi / length * phases
    weight = (0.5 - 0.5 * np.cos(2.0 * np.pi / length * samples)) / math.sqrt(length)
    rows = np.concatenate([np.cos(angles) * weight, -np.sin(angles) * weight])
    return rows.astype(np.float32).astype(jnp.bfloat16)


class Plan:
    def __init__(self, groups, pairs, items, channels):
        self.groups, self.pairs, self.items, self.channels = groups, pairs, items, channels
        self.depth = pairs // 4
        self.half = pairs // 2
        self.rows = min(8, items)
        self.pieces = items // self.rows
        self.bins = BINS // groups
        self.width = 2 * self.bins * channels
        middle = self.pieces // 2
        self.parts = [(k, 1) for k in range(self.pieces)]
        self.doubled = (min(3, len(self.parts) - 1), 0)


def gather_kernel(plan, blocks_hbm, map_hbm, table_hbm, records_ref, picked_ref,
                  stream, raw, own, spectra, maps, onehot, blocks_ref, table_ref,
                  load_sems, small_sems, recv_sems, twin_recv, z_send, side_send, twin_send,
                  tm_send, map_send, map_recv, keep_sems):
    groups, pairs, depth, half = plan.groups, plan.pairs, plan.depth, plan.half
    items, channels, length = records_ref.shape
    batch = stream.shape[1]
    depth_in = stream.shape[0]
    batches = items // batch
    per_piece = plan.rows // batch
    slots = blocks_ref.shape[2]
    t = lax.axis_index("tm")
    me = lax.axis_index("pairs")
    z = me // 4
    x = (me // 2) % 2
    c = me % 2
    place = x * depth + z
    up, down = me + 4, me - 4
    side = z * 4 + (1 - x) * 2 + c
    twin = z * 4 + x * 2 + 1 - c
    has_up = z < depth - 1
    has_down = z > 0
    out = 2 * (z // (depth // 2)) - 1

    def load(i):
        return pltpu.make_async_copy(
            records_ref.at[pl.ds(i * batch, batch)], stream.at[i % depth_in], load_sems.at[i % depth_in]
        )

    small = [
        pltpu.make_async_copy(table_hbm, table_ref, small_sems.at[0]),
        pltpu.make_async_copy(map_hbm, maps.at[t], small_sems.at[1]),
        pltpu.make_async_copy(blocks_hbm, blocks_ref, small_sems.at[2]),
    ]
    small[0].start()
    ahead = depth_in - 1
    for r in range(batch):
        pltpu.make_async_copy(records_ref.at[r], stream.at[0, r], load_sems.at[0]).start()
    for i in range(1, min(ahead, batches)):
        load(i).start()
    small[1].start()
    small[2].start()

    barrier = pltpu.get_barrier_semaphore()
    for d in range(1, groups):
        pl.semaphore_signal(barrier, inc=1, device_id=((t + d) % groups, me), device_id_type=MESH)
    for other in (side, twin):
        pl.semaphore_signal(barrier, inc=1, device_id=(t, other), device_id_type=MESH)

    @pl.when(has_up)
    def _():
        pl.semaphore_signal(barrier, inc=1, device_id=(t, up), device_id_type=MESH)

    @pl.when(has_down)
    def _():
        pl.semaphore_signal(barrier, inc=1, device_id=(t, down), device_id_type=MESH)

    def span(part):
        return pl.ds(*plan.parts[part])

    def landed(group, part, source):
        return spectra.at[group, span(part), c, source]

    def send(group, part, source, target, send_sem, recv_sem, kept):
        there = landed(group, part, source)
        return pltpu.make_async_remote_copy(
            src_ref=there if kept is None else kept,
            dst_ref=there,
            send_sem=send_sem,
            recv_sem=recv_sem,
            device_id=(t, target),
            device_id_type=MESH,
        )

    def to_twin(group, part, source, kept=None):
        send(group, part, source, twin, twin_send.at[0], twin_recv.at[group, part], kept).start()

    def spread(group, part, source, upward, downward, kept=None, across=True):
        recv = recv_sems.at[group, part, source]
        if across:
            send(group, part, source, side, side_send.at[group, part], recv, kept).start()
        if upward is not None:
            @pl.when(upward)
            def _():
                send(group, part, source, up, z_send.at[0, source], recv, kept).start()
        if downward is not None:
            @pl.when(downward)
            def _():
                send(group, part, source, down, z_send.at[1, source], recv, kept).start()
        to_twin(group, part, source, kept)

    def arrived(group, part, source):
        there = landed(group, part, source)
        pltpu.make_async_copy(there, there, recv_sems.at[group, part, source]).wait()

    def tm_copy(d, part):
        peer = (t + d) % groups
        return pltpu.make_async_remote_copy(
            src_ref=own.at[peer, span(part)],
            dst_ref=landed(t, part, place),
            send_sem=tm_send.at[d],
            recv_sem=recv_sems.at[t, part, place],
            device_id=(peer, me),
            device_id_type=MESH,
        )

    def map_copy(d):
        peer = (t + d) % groups
        return pltpu.make_async_remote_copy(
            src_ref=maps.at[t],
            dst_ref=maps.at[t],
            send_sem=map_send.at[d],
            recv_sem=map_recv.at[t],
            device_id=(peer, me),
            device_id_type=MESH,
        )

    def keep(k):
        return pltpu.make_async_copy(own.at[t, k], spectra.at[t, k, c, place], keep_sems.at[k])

    def from_tm(part):
        for d in range(1, groups):
            group = (t + d) % groups
            arrived(group, part, place)
            spread(group, part, place, has_up, has_down)

    def passed(toward, step, part, d, column, across):
        group = (t + d) % groups
        source = z + toward * step

        @pl.when((source >= 0) & (source < depth))
        def _():
            come = column + toward * step
            arrived(group, part, come)
            onward = z - toward

            @pl.when((onward >= 0) & (onward < depth))
            def _():
                send(group, part, come, me - 4 * toward, z_send.at[(1 + toward) // 2, come],
                     recv_sems.at[group, part, come], None).start()

            spread(group, part, come, None, None, None, across)

    def from_out(step, part, d, column=place, across=True):
        passed(out, step, part, d, column, across and (part, d) != plan.doubled)

    def from_in(step, part, d, column=place, across=True):
        passed(-out, step, part, d, column, across and (part, d) != plan.doubled)

    other = (1 - x) * depth + z

    def from_side(step, part, d):
        group = (t + d) % groups

        @pl.when(z - step >= 0)
        def _():
            arrived(group, part, other - step)
            to_twin(group, part, other - step)

        @pl.when((step > 0) & (z + step < depth))
        def _():
            arrived(group, part, other + step)
            to_twin(group, part, other + step)

    def doubled_start():
        part, d = plan.doubled
        group = (t + d) % groups
        arrived(group, part, other)
        spread(group, part, other, has_up, has_down, None, False)

    def launch(parts):
        for part in parts:
            for d in range(1, groups):
                tm_copy(d, part).start()
        for part in parts:
            spread(t, part, place, has_up, has_down, own.at[t, span(part)])

    total = maps.shape[2]

    def choose(group):
        wanted = lax.broadcasted_iota(jnp.int32, (WIN, total), 0) * NB
        lane = lax.broadcasted_iota(jnp.int32, (WIN, total), 1)
        offset = lane - wanted
        table = jnp.broadcast_to(maps[group], (WIN, total))
        owner = table // items
        line = (owner % 2 * plan.pieces + table % items // plan.rows) * 2 + (owner // 2) % 2
        line = (line * depth + owner // 4) * plan.rows + table % plan.rows
        for ref in range(2 * slots):
            block = jnp.broadcast_to(
                blocks_ref[0, ref % 2:ref % 2 + 1, ref // 2:ref // 2 + 1], (WIN, 1)
            )
            found = jnp.sum(jnp.where(offset == block, line, 0), axis=1, keepdims=True)
            found = jnp.where(block >= 0, found, -1)
            hit = (lane == found).astype(jnp.float32).astype(jnp.bfloat16)
            for core in range(2):
                lines = slice(core * (total // 2), (core + 1) * (total // 2))
                onehot[group, core, ref * WIN:(ref + 1) * WIN, :] = hit[:, lines]


    count = len(plan.parts)
    ready = {start + size - 1: part for part, (start, size) in enumerate(plan.parts)}
    far = range(1, groups)
    hooks = {}
    if batches == 8 and count == 4:
        hooks = {
            4: [(from_tm, 0), (from_out, 1, 0, 0)],
            5: [(from_in, 1, 0, 0)],
            6: [(from_tm, 1), (from_out, 1, 1, 0)],
        }
        steps = [(from_in, 1, 1, 0), (from_tm, 2)]
        first = [(0, d) for d in far] + [(2, 0)] + [(1, d) for d in far]
        steps += [(what, 1, part, d) for what in (from_out, from_in) for part, d in first]
        steps += [(from_tm, 3), (doubled_start,)]
        second = [(3, 0)] + [(part, d) for part in (2, 3) for d in far]
        steps += [(what, 1, part, d) for what in (from_out, from_in) for part, d in second]
    else:
        steps = [(from_tm, part) for part in range(count)] + [(doubled_start,)]
        for what in (from_out, from_in):
            steps += [(what, 1, part, d) for part in range(count) for d in range(groups)]

    def follow(some):
        for what, *which in some:
            what(*which)

    for k in range(plan.pieces):
        for j in range(per_piece):
            i = k * per_piece + j
            if i == 0:
                small[0].wait()
            load(i).wait()
            if i + ahead < batches:
                load(i + ahead).start()
            block = stream[i % depth_in].reshape(batch * channels, length)
            both = lax.dot_general(
                table_ref[...], block, (((1,), (1,)), ((), ())), preferred_element_type=jnp.float32
            )
            for r in range(batch):
                real = both[:BINS, r * channels:(r + 1) * channels]
                imag = both[BINS:, r * channels:(r + 1) * channels]
                power = jnp.mean(real * real + imag * imag, axis=1, keepdims=True)
                inverse = 1.0 / jnp.sqrt(power + 1e-06)
                raw[j * batch + r, :BINS] = real * inverse
                raw[j * batch + r, BINS:] = imag * inverse
            follow(hooks.get(i, []))
        turned = jnp.transpose(raw[...], (1, 0, 2)).astype(jnp.bfloat16)
        for h in range(groups):
            for part in range(2):
                for f in range(plan.bins):
                    col = (part * plan.bins + f) * channels
                    own[h, k, :, col:col + channels] = turned[part * BINS + h * plan.bins + f]
        if k == 0:
            pl.semaphore_wait(barrier, groups + 1 + has_up.astype(jnp.int32) + has_down.astype(jnp.int32))
            small[1].wait()
            for d in range(1, groups):
                map_copy(d).start()
        if k in ready:
            launch([ready[k]])
        keep(k).start()
    follow(steps)
    for k in range(plan.pieces):
        keep(k).wait()

    every = [(part, d) for part in range(count) for d in range(groups)]
    every.sort(key=lambda e: 2 * e[0] + 3 * e[1])
    crossing = [e for e in every if e != plan.doubled]

    @pl.loop(2, depth)
    def _(step):
        for what in (from_out, from_in):
            for part, d in every:
                what(step, part, d)
                if (part, d) == plan.doubled:
                    what(step - 1, part, d, other, False)
        for part, d in crossing:
            from_side(step - 2, part, d)

    for what in (from_out, from_in):
        what(depth - 1, *plan.doubled, other, False)

    small[2].wait()
    choose(t)

    for d in range(1, groups):
        group = (t + d) % groups
        pltpu.make_async_copy(maps.at[group], maps.at[group], map_recv.at[group]).wait()
        choose(group)
    def pick(group, core):
        rows_in = spectra[group, :, core].reshape(total // 2, plan.width)
        found = jnp.dot(onehot[group, core], rows_in, preferred_element_type=jnp.float32)
        return found.astype(jnp.bfloat16)

    for part, d in every:
        if (part, d) in crossing:
            if depth > 1:
                from_side(depth - 2, part, d)
            from_side(depth - 1, part, d)
    for d in range(groups):
        group = (t + d) % groups
        picked_ref[group] = pick(group, c)
    for d in range(groups):
        group = (t + d) % groups
        for part in range(count):
            there = spectra.at[group, span(part), 1 - c]
            pltpu.make_async_copy(there, there, twin_recv.at[group, part]).wait()
        picked_ref[group] = picked_ref[group] + pick(group, 1 - c)

    for d in range(1, groups):
        map_copy(d).wait_send()
        sent = own.at[(t + d) % groups]
        pltpu.make_async_copy(sent, sent, tm_send.at[d]).wait()

    for zz in range(depth):
        for column in (x, 1 - x):
            if depth == 1:
                continue
            source = column * depth + zz
            sent = spectra.at[:, :, c, source]
            if column is not x:
                sent = landed((t + plan.doubled[1]) % groups, plan.doubled[0], source)

            @pl.when(has_up & (zz <= z))
            def _():
                pltpu.make_async_copy(sent, sent, z_send.at[0, source]).wait()

            @pl.when(has_down & (zz >= z))
            def _():
                pltpu.make_async_copy(sent, sent, z_send.at[1, source]).wait()

    for part, d in every:
        group = (t + d) % groups
        sent = spectra.at[group, span(part), c, pl.ds(x * depth, depth)]
        if (part, d) == plan.doubled:
            sent = landed(group, part, place)
        pltpu.make_async_copy(sent, sent, side_send.at[group, part]).wait()
    sent = spectra.at[:, :, c]
    pltpu.make_async_copy(sent, sent, twin_send.at[0]).wait()


def gather_picked(plan, pair_blocks, source_map, table, records):
    items, channels, length = records.shape
    slots = pair_blocks.shape[1]
    groups, pairs = plan.groups, plan.pairs
    batch = min(4, plan.rows)
    streams = 3
    total = source_map.shape[1]
    dtype = jnp.bfloat16
    hbm = pl.BlockSpec(memory_space=pltpu.HBM)
    return pl.pallas_call(
        functools.partial(gather_kernel, plan),
        out_shape=jax.ShapeDtypeStruct((groups, 2 * slots * WIN, plan.width), dtype),
        in_specs=[hbm, hbm, hbm, hbm],
        out_specs=pl.BlockSpec(memory_space=pltpu.VMEM),
        scratch_shapes=[
            pltpu.VMEM((streams, batch, channels, length), dtype),
            pltpu.VMEM((plan.rows, 2 * BINS, channels), jnp.float32),
            pltpu.VMEM((groups, plan.pieces, plan.rows, plan.width), dtype),
            pltpu.VMEM((groups, plan.pieces, 2, plan.half, plan.rows, plan.width), dtype),
            pltpu.VMEM((groups,) + source_map.shape, jnp.int32),
            pltpu.VMEM((groups, 2, 2 * slots * WIN, total // 2), dtype),
            pltpu.VMEM((1, 2, slots), jnp.int32),
            pltpu.VMEM(table.shape, dtype),
            pltpu.SemaphoreType.DMA((streams,)),
            pltpu.SemaphoreType.DMA((3,)),
            pltpu.SemaphoreType.DMA((groups, len(plan.parts), plan.half)),
            pltpu.SemaphoreType.DMA((groups, len(plan.parts))),
            pltpu.SemaphoreType.DMA((2, plan.half)),
            pltpu.SemaphoreType.DMA((groups, len(plan.parts))),
            pltpu.SemaphoreType.DMA((1,)),
            pltpu.SemaphoreType.DMA((groups,)),
            pltpu.SemaphoreType.DMA((groups,)),
            pltpu.SemaphoreType.DMA((groups,)),
            pltpu.SemaphoreType.DMA((plan.pieces,)),
        ],
        compiler_params=pltpu.CompilerParams(
            collective_id=0, has_side_effects=True, vmem_limit_bytes=48 << 20
        ),
        name="gather_picked",
    )(
        pltpu.with_memory_space_constraint(jnp.transpose(pair_blocks, (0, 2, 1)), pltpu.HBM),
        pltpu.with_memory_space_constraint(source_map, pltpu.HBM),
        pltpu.with_memory_space_constraint(table, pltpu.HBM),
        records,
    )


def stack_kernel(plan, scale, picked_ref, out_ref, done, sems):
    groups = plan.groups
    slots, bins, _, channels, _ = out_ref.shape

    def write(s, f):
        return pltpu.make_async_copy(done.at[s, f], out_ref.at[s, f], sems.at[s, f])

    for s in range(slots):
        left = slice(2 * s * WIN, (2 * s + 1) * WIN)
        right = slice((2 * s + 1) * WIN, (2 * s + 2) * WIN)
        for f in range(bins):
            real = slice(f * channels, (f + 1) * channels)
            imag = slice((bins + f) * channels, (bins + f + 1) * channels)
            x_re = [picked_ref[g, left, real] for g in range(groups)]
            x_im = [picked_ref[g, left, imag] for g in range(groups)]
            y_re = jnp.concatenate([picked_ref[g, right, real] for g in range(groups)], axis=0)
            y_im = jnp.concatenate([picked_ref[g, right, imag] for g in range(groups)], axis=0)
            lhs = jnp.concatenate(x_re + x_im, axis=0)
            rhs = jnp.concatenate(
                [
                    jnp.concatenate([y_re, -y_im], axis=1),
                    jnp.concatenate([y_im, y_re], axis=1),
                ],
                axis=0,
            )
            both = lax.dot_general(
                lhs, rhs, (((0,), (0,)), ((), ())), preferred_element_type=jnp.float32
            )
            done[s, f, 0] = both[:, :channels] * scale
            done[s, f, 1] = both[:, channels:] * scale
            write(s, f).start()
    for s in range(slots):
        for f in range(bins):
            write(s, f).wait()


def stack_pairs(plan, slots, picked):
    channels, bins = plan.channels, plan.bins
    scale = 1.0 / math.sqrt(WIN * plan.groups)
    vmem = pl.BlockSpec(memory_space=pltpu.VMEM)
    shape = (slots, bins, 2, channels, channels)
    return pl.pallas_call(
        functools.partial(stack_kernel, plan, scale),
        out_shape=jax.ShapeDtypeStruct(shape, jnp.float32),
        in_specs=[vmem],
        out_specs=pl.BlockSpec(memory_space=pl.ANY),
        scratch_shapes=[pltpu.VMEM(shape, jnp.float32), pltpu.SemaphoreType.DMA((slots, bins))],
        compiler_params=pltpu.CompilerParams(vmem_limit_bytes=40 << 20),
        name="stack_pairs",
    )(picked)


def per_device(groups, pairs, records, source_map, pair_blocks):
    table = jnp.asarray(transform_table(records.shape[3]))
    plan = Plan(groups, pairs, records.shape[1], records.shape[2])
    picked = gather_picked(plan, pair_blocks, source_map, table, records[0])
    return stack_pairs(plan, pair_blocks.shape[1], picked)


def solution(mesh):
    groups, pairs = mesh.shape["tm"], mesh.shape["pairs"]
    return jax.shard_map(
        functools.partial(per_device, groups, pairs),
        mesh=mesh,
        in_specs=(P("tm", "pairs", None, None), P("tm", None), P("pairs", None, None)),
        out_specs=P("pairs", "tm", None, None, None),
        check_vma=False,
    )
```

```python
import functools
import math

import jax
import jax.numpy as jnp
import numpy as np
from jax import lax
from jax.experimental import pallas as pl
from jax.experimental.pallas import tpu as pltpu
from jax.sharding import PartitionSpec as P

NB = 32
BINS = 16
FIRST_BIN = 64
WIN = 16
MESH = pl.DeviceIdType.MESH


def transform_table(length):
    samples = np.arange(length)
    phases = samples[None, :] * (FIRST_BIN + np.arange(BINS))[:, None] % length
    angles = 2.0 * np.pi / length * phases
    weight = (0.5 - 0.5 * np.cos(2.0 * np.pi / length * samples)) / math.sqrt(length)
    rows = np.concatenate([np.cos(angles) * weight, -np.sin(angles) * weight])
    return rows.astype(np.float32).astype(jnp.bfloat16)


class Plan:
    def __init__(self, groups, pairs, items, channels):
        self.groups, self.pairs, self.items, self.channels = groups, pairs, items, channels
        self.depth = pairs // 4
        self.half = pairs // 2
        self.rows = min(8, items)
        self.pieces = items // self.rows
        self.bins = BINS // groups
        self.width = 2 * self.bins * channels
        middle = self.pieces // 2
        self.parts = [(k, 1) for k in range(self.pieces)]
        self.doubled = (min(2, len(self.parts) - 1), 0)


def gather_kernel(plan, blocks_hbm, map_hbm, table_hbm, records_ref, picked_ref,
                  stream, raw, own, spectra, maps, onehot, blocks_ref, table_ref,
                  load_sems, small_sems, recv_sems, twin_recv, z_send, side_send, twin_send,
                  tm_send, map_send, map_recv, keep_sems):
    groups, pairs, depth, half = plan.groups, plan.pairs, plan.depth, plan.half
    items, channels, length = records_ref.shape
    batch = stream.shape[1]
    depth_in = stream.shape[0]
    batches = items // batch
    per_piece = plan.rows // batch
    slots = blocks_ref.shape[2]
    t = lax.axis_index("tm")
    me = lax.axis_index("pairs")
    z = me // 4
    x = (me // 2) % 2
    c = me % 2
    place = x * depth + z
    up, down = me + 4, me - 4
    side = z * 4 + (1 - x) * 2 + c
    twin = z * 4 + x * 2 + 1 - c
    has_up = z < depth - 1
    has_down = z > 0
    out = 2 * (z // (depth // 2)) - 1

    def load(i):
        return pltpu.make_async_copy(
            records_ref.at[pl.ds(i * batch, batch)], stream.at[i % depth_in], load_sems.at[i % depth_in]
        )

    small = [
        pltpu.make_async_copy(table_hbm, table_ref, small_sems.at[0]),
        pltpu.make_async_copy(map_hbm, maps.at[t], small_sems.at[1]),
        pltpu.make_async_copy(blocks_hbm, blocks_ref, small_sems.at[2]),
    ]
    small[0].start()
    ahead = depth_in - 1
    for r in range(batch):
        pltpu.make_async_copy(records_ref.at[r], stream.at[0, r], load_sems.at[0]).start()
    for i in range(1, min(ahead, batches)):
        load(i).start()
    small[1].start()
    small[2].start()

    barrier = pltpu.get_barrier_semaphore()
    for d in range(1, groups):
        pl.semaphore_signal(barrier, inc=1, device_id=((t + d) % groups, me), device_id_type=MESH)
    for other in (side, twin):
        pl.semaphore_signal(barrier, inc=1, device_id=(t, other), device_id_type=MESH)

    @pl.when(has_up)
    def _():
        pl.semaphore_signal(barrier, inc=1, device_id=(t, up), device_id_type=MESH)

    @pl.when(has_down)
    def _():
        pl.semaphore_signal(barrier, inc=1, device_id=(t, down), device_id_type=MESH)

    def span(part):
        return pl.ds(*plan.parts[part])

    def landed(group, part, source):
        return spectra.at[group, span(part), c, source]

    def send(group, part, source, target, send_sem, recv_sem, kept):
        there = landed(group, part, source)
        return pltpu.make_async_remote_copy(
            src_ref=there if kept is None else kept,
            dst_ref=there,
            send_sem=send_sem,
            recv_sem=recv_sem,
            device_id=(t, target),
            device_id_type=MESH,
        )

    def to_twin(group, part, source, kept=None):
        send(group, part, source, twin, twin_send.at[0], twin_recv.at[group, part], kept).start()

    def spread(group, part, source, upward, downward, kept=None, across=True):
        recv = recv_sems.at[group, part, source]
        if across:
            send(group, part, source, side, side_send.at[group, part], recv, kept).start()
        if upward is not None:
            @pl.when(upward)
            def _():
                send(group, part, source, up, z_send.at[0, source], recv, kept).start()
        if downward is not None:
            @pl.when(downward)
            def _():
                send(group, part, source, down, z_send.at[1, source], recv, kept).start()
        to_twin(group, part, source, kept)

    def arrived(group, part, source):
        there = landed(group, part, source)
        pltpu.make_async_copy(there, there, recv_sems.at[group, part, source]).wait()

    def tm_copy(d, part):
        peer = (t + d) % groups
        return pltpu.make_async_remote_copy(
            src_ref=own.at[peer, span(part)],
            dst_ref=landed(t, part, place),
            send_sem=tm_send.at[d],
            recv_sem=recv_sems.at[t, part, place],
            device_id=(peer, me),
            device_id_type=MESH,
        )

    def map_copy(d):
        peer = (t + d) % groups
        return pltpu.make_async_remote_copy(
            src_ref=maps.at[t],
            dst_ref=maps.at[t],
            send_sem=map_send.at[d],
            recv_sem=map_recv.at[t],
            device_id=(peer, me),
            device_id_type=MESH,
        )

    def keep(k):
        return pltpu.make_async_copy(own.at[t, k], spectra.at[t, k, c, place], keep_sems.at[k])

    def from_tm(part):
        for d in range(1, groups):
            group = (t + d) % groups
            arrived(group, part, place)
            spread(group, part, place, has_up, has_down)

    def passed(toward, step, part, d, column, across):
        group = (t + d) % groups
        source = z + toward * step

        @pl.when((source >= 0) & (source < depth))
        def _():
            come = column + toward * step
            arrived(group, part, come)
            onward = z - toward

            @pl.when((onward >= 0) & (onward < depth))
            def _():
                send(group, part, come, me - 4 * toward, z_send.at[(1 + toward) // 2, come],
                     recv_sems.at[group, part, come], None).start()

            spread(group, part, come, None, None, None, across)

    def from_out(step, part, d, column=place, across=True):
        passed(out, step, part, d, column, across and (part, d) != plan.doubled)

    def from_in(step, part, d, column=place, across=True):
        passed(-out, step, part, d, column, across and (part, d) != plan.doubled)

    other = (1 - x) * depth + z

    def from_side(step, part, d):
        group = (t + d) % groups

        @pl.when(z - step >= 0)
        def _():
            arrived(group, part, other - step)
            to_twin(group, part, other - step)

        @pl.when((step > 0) & (z + step < depth))
        def _():
            arrived(group, part, other + step)
            to_twin(group, part, other + step)

    def doubled_start():
        part, d = plan.doubled
        group = (t + d) % groups
        arrived(group, part, other)
        spread(group, part, other, has_up, has_down, None, False)

    def launch(parts):
        for part in parts:
            for d in range(1, groups):
                tm_copy(d, part).start()
        for part in parts:
            spread(t, part, place, has_up, has_down, own.at[t, span(part)])

    total = maps.shape[2]

    def choose(group):
        wanted = lax.broadcasted_iota(jnp.int32, (WIN, total), 0) * NB
        lane = lax.broadcasted_iota(jnp.int32, (WIN, total), 1)
        offset = lane - wanted
        table = jnp.broadcast_to(maps[group], (WIN, total))
        owner = table // items
        line = (owner % 2 * plan.pieces + table % items // plan.rows) * 2 + (owner // 2) % 2
        line = (line * depth + owner // 4) * plan.rows + table % plan.rows
        for ref in range(2 * slots):
            block = jnp.broadcast_to(
                blocks_ref[0, ref % 2:ref % 2 + 1, ref // 2:ref // 2 + 1], (WIN, 1)
            )
            found = jnp.sum(jnp.where(offset == block, line, 0), axis=1, keepdims=True)
            found = jnp.where(block >= 0, found, -1)
            hit = (lane == found).astype(jnp.float32).astype(jnp.bfloat16)
            for core in range(2):
                lines = slice(core * (total // 2), (core + 1) * (total // 2))
                onehot[group, core, ref * WIN:(ref + 1) * WIN, :] = hit[:, lines]


    count = len(plan.parts)
    ready = {start + size - 1: part for part, (start, size) in enumerate(plan.parts)}
    far = range(1, groups)
    hooks = {}
    if batches == 8 and count == 4:
        hooks = {
            4: [(from_tm, 0), (from_out, 1, 0, 0)],
            5: [(from_in, 1, 0, 0)],
            6: [(from_tm, 1), (from_out, 1, 1, 0)],
        }
        steps = [(from_in, 1, 1, 0), (from_tm, 2)]
        first = [(0, d) for d in far] + [(2, 0)] + [(1, d) for d in far]
        steps += [(what, 1, part, d) for what in (from_out, from_in) for part, d in first]
        steps += [(doubled_start,), (from_tm, 3)]
        second = [(3, 0)] + [(part, d) for part in (2, 3) for d in far]
        steps += [(what, 1, part, d) for what in (from_out, from_in) for part, d in second]
    else:
        steps = [(from_tm, part) for part in range(count)] + [(doubled_start,)]
        for what in (from_out, from_in):
            steps += [(what, 1, part, d) for part in range(count) for d in range(groups)]

    def follow(some):
        for what, *which in some:
            what(*which)

    for k in range(plan.pieces):
        for j in range(per_piece):
            i = k * per_piece + j
            if i == 0:
                small[0].wait()
            load(i).wait()
            if i + ahead < batches:
                load(i + ahead).start()
            block = stream[i % depth_in].reshape(batch * channels, length)
            both = lax.dot_general(
                table_ref[...], block, (((1,), (1,)), ((), ())), preferred_element_type=jnp.float32
            )
            for r in range(batch):
                real = both[:BINS, r * channels:(r + 1) * channels]
                imag = both[BINS:, r * channels:(r + 1) * channels]
                power = jnp.mean(real * real + imag * imag, axis=1, keepdims=True)
                inverse = 1.0 / jnp.sqrt(power + 1e-06)
                raw[j * batch + r, :BINS] = real * inverse
                raw[j * batch + r, BINS:] = imag * inverse
            follow(hooks.get(i, []))
        turned = jnp.transpose(raw[...], (1, 0, 2)).astype(jnp.bfloat16)
        for h in range(groups):
            for part in range(2):
                for f in range(plan.bins):
                    col = (part * plan.bins + f) * channels
                    own[h, k, :, col:col + channels] = turned[part * BINS + h * plan.bins + f]
        if k == 0:
            pl.semaphore_wait(barrier, groups + 1 + has_up.astype(jnp.int32) + has_down.astype(jnp.int32))
            small[1].wait()
            for d in range(1, groups):
                map_copy(d).start()
        if k in ready:
            launch([ready[k]])
        keep(k).start()
    follow(steps)
    for k in range(plan.pieces):
        keep(k).wait()

    every = [(part, d) for part in range(count) for d in range(groups)]
    every.sort(key=lambda e: 2 * e[0] + 3 * e[1])
    crossing = [e for e in every if e != plan.doubled]

    @pl.loop(2, depth)
    def _(step):
        for what in (from_out, from_in):
            for part, d in every:
                what(step, part, d)
                if (part, d) == plan.doubled:
                    what(step - 1, part, d, other, False)
        for part, d in crossing:
            from_side(step - 2, part, d)

    for what in (from_out, from_in):
        what(depth - 1, *plan.doubled, other, False)

    small[2].wait()
    choose(t)

    for d in range(1, groups):
        group = (t + d) % groups
        pltpu.make_async_copy(maps.at[group], maps.at[group], map_recv.at[group]).wait()
        choose(group)
    def pick(group, core):
        rows_in = spectra[group, :, core].reshape(total // 2, plan.width)
        found = jnp.dot(onehot[group, core], rows_in, preferred_element_type=jnp.float32)
        return found.astype(jnp.bfloat16)

    for part, d in every:
        if (part, d) in crossing:
            if depth > 1:
                from_side(depth - 2, part, d)
            from_side(depth - 1, part, d)
    for d in range(groups):
        group = (t + d) % groups
        picked_ref[group] = pick(group, c)
    for d in range(groups):
        group = (t + d) % groups
        for part in range(count):
            there = spectra.at[group, span(part), 1 - c]
            pltpu.make_async_copy(there, there, twin_recv.at[group, part]).wait()
        picked_ref[group] = picked_ref[group] + pick(group, 1 - c)

    for d in range(1, groups):
        map_copy(d).wait_send()
        sent = own.at[(t + d) % groups]
        pltpu.make_async_copy(sent, sent, tm_send.at[d]).wait()

    for zz in range(depth):
        for column in (x, 1 - x):
            if depth == 1:
                continue
            source = column * depth + zz
            sent = spectra.at[:, :, c, source]
            if column is not x:
                sent = landed((t + plan.doubled[1]) % groups, plan.doubled[0], source)

            @pl.when(has_up & (zz <= z))
            def _():
                pltpu.make_async_copy(sent, sent, z_send.at[0, source]).wait()

            @pl.when(has_down & (zz >= z))
            def _():
                pltpu.make_async_copy(sent, sent, z_send.at[1, source]).wait()

    for part, d in every:
        group = (t + d) % groups
        sent = spectra.at[group, span(part), c, pl.ds(x * depth, depth)]
        if (part, d) == plan.doubled:
            sent = landed(group, part, place)
        pltpu.make_async_copy(sent, sent, side_send.at[group, part]).wait()
    sent = spectra.at[:, :, c]
    pltpu.make_async_copy(sent, sent, twin_send.at[0]).wait()


def gather_picked(plan, pair_blocks, source_map, table, records):
    items, channels, length = records.shape
    slots = pair_blocks.shape[1]
    groups, pairs = plan.groups, plan.pairs
    batch = min(4, plan.rows)
    streams = 3
    total = source_map.shape[1]
    dtype = jnp.bfloat16
    hbm = pl.BlockSpec(memory_space=pltpu.HBM)
    return pl.pallas_call(
        functools.partial(gather_kernel, plan),
        out_shape=jax.ShapeDtypeStruct((groups, 2 * slots * WIN, plan.width), dtype),
        in_specs=[hbm, hbm, hbm, hbm],
        out_specs=pl.BlockSpec(memory_space=pltpu.VMEM),
        scratch_shapes=[
            pltpu.VMEM((streams, batch, channels, length), dtype),
            pltpu.VMEM((plan.rows, 2 * BINS, channels), jnp.float32),
            pltpu.VMEM((groups, plan.pieces, plan.rows, plan.width), dtype),
            pltpu.VMEM((groups, plan.pieces, 2, plan.half, plan.rows, plan.width), dtype),
            pltpu.VMEM((groups,) + source_map.shape, jnp.int32),
            pltpu.VMEM((groups, 2, 2 * slots * WIN, total // 2), dtype),
            pltpu.VMEM((1, 2, slots), jnp.int32),
            pltpu.VMEM(table.shape, dtype),
            pltpu.SemaphoreType.DMA((streams,)),
            pltpu.SemaphoreType.DMA((3,)),
            pltpu.SemaphoreType.DMA((groups, len(plan.parts), plan.half)),
            pltpu.SemaphoreType.DMA((groups, len(plan.parts))),
            pltpu.SemaphoreType.DMA((2, plan.half)),
            pltpu.SemaphoreType.DMA((groups, len(plan.parts))),
            pltpu.SemaphoreType.DMA((1,)),
            pltpu.SemaphoreType.DMA((groups,)),
            pltpu.SemaphoreType.DMA((groups,)),
            pltpu.SemaphoreType.DMA((groups,)),
            pltpu.SemaphoreType.DMA((plan.pieces,)),
        ],
        compiler_params=pltpu.CompilerParams(
            collective_id=0, has_side_effects=True, vmem_limit_bytes=48 << 20
        ),
        name="gather_picked",
    )(
        pltpu.with_memory_space_constraint(jnp.transpose(pair_blocks, (0, 2, 1)), pltpu.HBM),
        pltpu.with_memory_space_constraint(source_map, pltpu.HBM),
        pltpu.with_memory_space_constraint(table, pltpu.HBM),
        records,
    )


def stack_kernel(plan, scale, picked_ref, out_ref, done, sems):
    groups = plan.groups
    slots, bins, _, channels, _ = out_ref.shape

    def write(s, f):
        return pltpu.make_async_copy(done.at[s, f], out_ref.at[s, f], sems.at[s, f])

    for s in range(slots):
        left = slice(2 * s * WIN, (2 * s + 1) * WIN)
        right = slice((2 * s + 1) * WIN, (2 * s + 2) * WIN)
        for f in range(bins):
            real = slice(f * channels, (f + 1) * channels)
            imag = slice((bins + f) * channels, (bins + f + 1) * channels)
            x_re = [picked_ref[g, left, real] for g in range(groups)]
            x_im = [picked_ref[g, left, imag] for g in range(groups)]
            y_re = jnp.concatenate([picked_ref[g, right, real] for g in range(groups)], axis=0)
            y_im = jnp.concatenate([picked_ref[g, right, imag] for g in range(groups)], axis=0)
            lhs = jnp.concatenate(x_re + x_im, axis=0)
            rhs = jnp.concatenate(
                [
                    jnp.concatenate([y_re, -y_im], axis=1),
                    jnp.concatenate([y_im, y_re], axis=1),
                ],
                axis=0,
            )
            both = lax.dot_general(
                lhs, rhs, (((0,), (0,)), ((), ())), preferred_element_type=jnp.float32
            )
            done[s, f, 0] = both[:, :channels] * scale
            done[s, f, 1] = both[:, channels:] * scale
            write(s, f).start()
    for s in range(slots):
        for f in range(bins):
            write(s, f).wait()


def stack_pairs(plan, slots, picked):
    channels, bins = plan.channels, plan.bins
    scale = 1.0 / math.sqrt(WIN * plan.groups)
    vmem = pl.BlockSpec(memory_space=pltpu.VMEM)
    shape = (slots, bins, 2, channels, channels)
    return pl.pallas_call(
        functools.partial(stack_kernel, plan, scale),
        out_shape=jax.ShapeDtypeStruct(shape, jnp.float32),
        in_specs=[vmem],
        out_specs=pl.BlockSpec(memory_space=pl.ANY),
        scratch_shapes=[pltpu.VMEM(shape, jnp.float32), pltpu.SemaphoreType.DMA((slots, bins))],
        compiler_params=pltpu.CompilerParams(vmem_limit_bytes=40 << 20),
        name="stack_pairs",
    )(picked)


def per_device(groups, pairs, records, source_map, pair_blocks):
    table = jnp.asarray(transform_table(records.shape[3]))
    plan = Plan(groups, pairs, records.shape[1], records.shape[2])
    picked = gather_picked(plan, pair_blocks, source_map, table, records[0])
    return stack_pairs(plan, pair_blocks.shape[1], picked)


def solution(mesh):
    groups, pairs = mesh.shape["tm"], mesh.shape["pairs"]
    return jax.shard_map(
        functools.partial(per_device, groups, pairs),
        mesh=mesh,
        in_specs=(P("tm", "pairs", None, None), P("tm", None), P("pairs", None, None)),
        out_specs=P("pairs", "tm", None, None, None),
        check_vma=False,
    )
```

```python
import functools
import math

import jax
import jax.numpy as jnp
import numpy as np
from jax import lax
from jax.experimental import pallas as pl
from jax.experimental.pallas import tpu as pltpu
from jax.sharding import PartitionSpec as P

NB = 32
BINS = 16
FIRST_BIN = 64
WIN = 16
MESH = pl.DeviceIdType.MESH


def transform_table(length):
    samples = np.arange(length)
    phases = samples[None, :] * (FIRST_BIN + np.arange(BINS))[:, None] % length
    angles = 2.0 * np.pi / length * phases
    weight = (0.5 - 0.5 * np.cos(2.0 * np.pi / length * samples)) / math.sqrt(length)
    rows = np.concatenate([np.cos(angles) * weight, -np.sin(angles) * weight])
    return rows.astype(np.float32).astype(jnp.bfloat16)


class Plan:
    def __init__(self, groups, pairs, items, channels):
        self.groups, self.pairs, self.items, self.channels = groups, pairs, items, channels
        self.depth = pairs // 4
        self.half = pairs // 2
        self.rows = min(8, items)
        self.pieces = items // self.rows
        self.bins = BINS // groups
        self.width = 2 * self.bins * channels
        middle = self.pieces // 2
        self.parts = [(k, 1) for k in range(self.pieces)]
        self.doubled = (min(3, len(self.parts) - 1), 0)


def gather_kernel(plan, blocks_hbm, map_hbm, table_hbm, records_ref, picked_ref,
                  stream, raw, own, spectra, maps, onehot, blocks_ref, table_ref,
                  load_sems, small_sems, recv_sems, twin_recv, z_send, side_send, twin_send,
                  tm_send, map_send, map_recv, keep_sems):
    groups, pairs, depth, half = plan.groups, plan.pairs, plan.depth, plan.half
    items, channels, length = records_ref.shape
    batch = stream.shape[1]
    depth_in = stream.shape[0]
    batches = items // batch
    per_piece = plan.rows // batch
    slots = blocks_ref.shape[2]
    t = lax.axis_index("tm")
    me = lax.axis_index("pairs")
    z = me // 4
    x = (me // 2) % 2
    c = me % 2
    place = x * depth + z
    up, down = me + 4, me - 4
    side = z * 4 + (1 - x) * 2 + c
    twin = z * 4 + x * 2 + 1 - c
    has_up = z < depth - 1
    has_down = z > 0
    out = 2 * (z // (depth // 2)) - 1

    def load(i):
        return pltpu.make_async_copy(
            records_ref.at[pl.ds(i * batch, batch)], stream.at[i % depth_in], load_sems.at[i % depth_in]
        )

    small = [
        pltpu.make_async_copy(table_hbm, table_ref, small_sems.at[0]),
        pltpu.make_async_copy(map_hbm, maps.at[t], small_sems.at[1]),
        pltpu.make_async_copy(blocks_hbm, blocks_ref, small_sems.at[2]),
    ]
    small[0].start()
    ahead = depth_in - 1
    for r in range(batch):
        pltpu.make_async_copy(records_ref.at[r], stream.at[0, r], load_sems.at[0]).start()
    for i in range(1, min(ahead, batches)):
        load(i).start()
    small[1].start()
    small[2].start()

    barrier = pltpu.get_barrier_semaphore()
    for d in range(1, groups):
        pl.semaphore_signal(barrier, inc=1, device_id=((t + d) % groups, me), device_id_type=MESH)
    for other in (side, twin):
        pl.semaphore_signal(barrier, inc=1, device_id=(t, other), device_id_type=MESH)

    @pl.when(has_up)
    def _():
        pl.semaphore_signal(barrier, inc=1, device_id=(t, up), device_id_type=MESH)

    @pl.when(has_down)
    def _():
        pl.semaphore_signal(barrier, inc=1, device_id=(t, down), device_id_type=MESH)

    def span(part):
        return pl.ds(*plan.parts[part])

    def landed(group, part, source):
        return spectra.at[group, span(part), c, source]

    def send(group, part, source, target, send_sem, recv_sem, kept):
        there = landed(group, part, source)
        return pltpu.make_async_remote_copy(
            src_ref=there if kept is None else kept,
            dst_ref=there,
            send_sem=send_sem,
            recv_sem=recv_sem,
            device_id=(t, target),
            device_id_type=MESH,
        )

    def to_twin(group, part, source, kept=None):
        send(group, part, source, twin, twin_send.at[0], twin_recv.at[group, part], kept).start()

    def spread(group, part, source, upward, downward, kept=None, across=True):
        recv = recv_sems.at[group, part, source]
        if across:
            send(group, part, source, side, side_send.at[group, part], recv, kept).start()
        if upward is not None:
            @pl.when(upward)
            def _():
                send(group, part, source, up, z_send.at[0, source], recv, kept).start()
        if downward is not None:
            @pl.when(downward)
            def _():
                send(group, part, source, down, z_send.at[1, source], recv, kept).start()
        to_twin(group, part, source, kept)

    def arrived(group, part, source):
        there = landed(group, part, source)
        pltpu.make_async_copy(there, there, recv_sems.at[group, part, source]).wait()

    def tm_copy(d, part):
        peer = (t + d) % groups
        return pltpu.make_async_remote_copy(
            src_ref=own.at[peer, span(part)],
            dst_ref=landed(t, part, place),
            send_sem=tm_send.at[d],
            recv_sem=recv_sems.at[t, part, place],
            device_id=(peer, me),
            device_id_type=MESH,
        )

    def map_copy(d):
        peer = (t + d) % groups
        return pltpu.make_async_remote_copy(
            src_ref=maps.at[t],
            dst_ref=maps.at[t],
            send_sem=map_send.at[d],
            recv_sem=map_recv.at[t],
            device_id=(peer, me),
            device_id_type=MESH,
        )

    def keep(k):
        return pltpu.make_async_copy(own.at[t, k], spectra.at[t, k, c, place], keep_sems.at[k])

    def from_tm(part):
        for d in range(1, groups):
            group = (t + d) % groups
            arrived(group, part, place)
            spread(group, part, place, has_up, has_down)

    def passed(toward, step, part, d, column, across):
        group = (t + d) % groups
        source = z + toward * step

        @pl.when((source >= 0) & (source < depth))
        def _():
            come = column + toward * step
            arrived(group, part, come)
            onward = z - toward

            @pl.when((onward >= 0) & (onward < depth))
            def _():
                send(group, part, come, me - 4 * toward, z_send.at[(1 + toward) // 2, come],
                     recv_sems.at[group, part, come], None).start()

            spread(group, part, come, None, None, None, across)

    def from_out(step, part, d, column=place, across=True):
        passed(out, step, part, d, column, across and (part, d) != plan.doubled)

    def from_in(step, part, d, column=place, across=True):
        passed(-out, step, part, d, column, across and (part, d) != plan.doubled)

    other = (1 - x) * depth + z

    def from_side(step, part, d):
        group = (t + d) % groups

        @pl.when(z - step >= 0)
        def _():
            arrived(group, part, other - step)
            to_twin(group, part, other - step)

        @pl.when((step > 0) & (z + step < depth))
        def _():
            arrived(group, part, other + step)
            to_twin(group, part, other + step)

    def doubled_start():
        part, d = plan.doubled
        group = (t + d) % groups
        arrived(group, part, other)
        spread(group, part, other, has_up, has_down, None, False)

    def launch(parts):
        for part in parts:
            for d in range(1, groups):
                tm_copy(d, part).start()
        for part in parts:
            spread(t, part, place, has_up, has_down, own.at[t, span(part)])

    total = maps.shape[2]

    def choose(group):
        wanted = lax.broadcasted_iota(jnp.int32, (WIN, total), 0) * NB
        lane = lax.broadcasted_iota(jnp.int32, (WIN, total), 1)
        offset = lane - wanted
        table = jnp.broadcast_to(maps[group], (WIN, total))
        owner = table // items
        line = (owner % 2 * plan.pieces + table % items // plan.rows) * 2 + (owner // 2) % 2
        line = (line * depth + owner // 4) * plan.rows + table % plan.rows
        for ref in range(2 * slots):
            block = jnp.broadcast_to(
                blocks_ref[0, ref % 2:ref % 2 + 1, ref // 2:ref // 2 + 1], (WIN, 1)
            )
            found = jnp.sum(jnp.where(offset == block, line, 0), axis=1, keepdims=True)
            found = jnp.where(block >= 0, found, -1)
            hit = (lane == found).astype(jnp.float32).astype(jnp.bfloat16)
            for core in range(2):
                lines = slice(core * (total // 2), (core + 1) * (total // 2))
                onehot[group, core, ref * WIN:(ref + 1) * WIN, :] = hit[:, lines]


    count = len(plan.parts)
    ready = {start + size - 1: part for part, (start, size) in enumerate(plan.parts)}
    far = range(1, groups)
    hooks = {}
    if batches == 8 and count == 4:
        hooks = {
            4: [(from_tm, 0), (from_out, 1, 0, 0)],
            5: [(from_in, 1, 0, 0)],
            6: [(from_tm, 1), (from_out, 1, 1, 0)],
        }
        steps = [(from_in, 1, 1, 0), (from_tm, 2)]
        first = [(0, d) for d in far] + [(2, 0)] + [(1, d) for d in far]
        steps += [(what, 1, part, d) for what in (from_out, from_in) for part, d in first]
        steps += [(from_tm, 3), (doubled_start,)]
        second = [(3, 0)] + [(part, d) for part in (2, 3) for d in far]
        steps += [(what, 1, part, d) for what in (from_out, from_in) for part, d in second]
    else:
        steps = [(from_tm, part) for part in range(count)] + [(doubled_start,)]
        for what in (from_out, from_in):
            steps += [(what, 1, part, d) for part in range(count) for d in range(groups)]

    def follow(some):
        for what, *which in some:
            what(*which)

    for k in range(plan.pieces):
        for j in range(per_piece):
            i = k * per_piece + j
            if i == 0:
                small[0].wait()
            load(i).wait()
            if i + ahead < batches:
                load(i + ahead).start()
            block = stream[i % depth_in].reshape(batch * channels, length)
            both = lax.dot_general(
                table_ref[...], block, (((1,), (1,)), ((), ())), preferred_element_type=jnp.float32
            )
            for r in range(batch):
                real = both[:BINS, r * channels:(r + 1) * channels]
                imag = both[BINS:, r * channels:(r + 1) * channels]
                power = jnp.mean(real * real + imag * imag, axis=1, keepdims=True)
                inverse = 1.0 / jnp.sqrt(power + 1e-06)
                raw[j * batch + r, :BINS] = real * inverse
                raw[j * batch + r, BINS:] = imag * inverse
            follow(hooks.get(i, []))
        turned = jnp.transpose(raw[...], (1, 0, 2)).astype(jnp.bfloat16)
        for h in range(groups):
            for part in range(2):
                for f in range(plan.bins):
                    col = (part * plan.bins + f) * channels
                    own[h, k, :, col:col + channels] = turned[part * BINS + h * plan.bins + f]
        if k == 0:
            pl.semaphore_wait(barrier, groups + 1 + has_up.astype(jnp.int32) + has_down.astype(jnp.int32))
            small[1].wait()
            for d in range(1, groups):
                map_copy(d).start()
        if k in ready:
            launch([ready[k]])
        keep(k).start()
    follow(steps)
    for k in range(plan.pieces):
        keep(k).wait()

    every = [(part, d) for part in range(count) for d in range(groups)]
    every.sort(key=lambda e: 2 * e[0] + 3 * e[1])
    crossing = [e for e in every if e != plan.doubled]

    @pl.loop(2, depth)
    def _(step):
        for what in (from_out, from_in):
            for part, d in every:
                what(step, part, d)
                if (part, d) == plan.doubled:
                    what(step - 1, part, d, other, False)

    @pl.loop(0, depth - 2)
    def _(step):
        for part, d in crossing:
            from_side(step, part, d)

    for what in (from_out, from_in):
        what(depth - 1, *plan.doubled, other, False)

    small[2].wait()
    choose(t)

    for d in range(1, groups):
        group = (t + d) % groups
        pltpu.make_async_copy(maps.at[group], maps.at[group], map_recv.at[group]).wait()
        choose(group)
    def pick(group, core):
        rows_in = spectra[group, :, core].reshape(total // 2, plan.width)
        found = jnp.dot(onehot[group, core], rows_in, preferred_element_type=jnp.float32)
        return found.astype(jnp.bfloat16)

    for part, d in every:
        if (part, d) in crossing:
            if depth > 1:
                from_side(depth - 2, part, d)
            from_side(depth - 1, part, d)
    for d in range(groups):
        group = (t + d) % groups
        picked_ref[group] = pick(group, c)
    for d in range(groups):
        group = (t + d) % groups
        for part in range(count):
            there = spectra.at[group, span(part), 1 - c]
            pltpu.make_async_copy(there, there, twin_recv.at[group, part]).wait()
        picked_ref[group] = picked_ref[group] + pick(group, 1 - c)

    for d in range(1, groups):
        map_copy(d).wait_send()
        sent = own.at[(t + d) % groups]
        pltpu.make_async_copy(sent, sent, tm_send.at[d]).wait()

    for zz in range(depth):
        for column in (x, 1 - x):
            if depth == 1:
                continue
            source = column * depth + zz
            sent = spectra.at[:, :, c, source]
            if column is not x:
                sent = landed((t + plan.doubled[1]) % groups, plan.doubled[0], source)

            @pl.when(has_up & (zz <= z))
            def _():
                pltpu.make_async_copy(sent, sent, z_send.at[0, source]).wait()

            @pl.when(has_down & (zz >= z))
            def _():
                pltpu.make_async_copy(sent, sent, z_send.at[1, source]).wait()

    for part, d in every:
        group = (t + d) % groups
        sent = spectra.at[group, span(part), c, pl.ds(x * depth, depth)]
        if (part, d) == plan.doubled:
            sent = landed(group, part, place)
        pltpu.make_async_copy(sent, sent, side_send.at[group, part]).wait()
    sent = spectra.at[:, :, c]
    pltpu.make_async_copy(sent, sent, twin_send.at[0]).wait()


def gather_picked(plan, pair_blocks, source_map, table, records):
    items, channels, length = records.shape
    slots = pair_blocks.shape[1]
    groups, pairs = plan.groups, plan.pairs
    batch = min(4, plan.rows)
    streams = 3
    total = source_map.shape[1]
    dtype = jnp.bfloat16
    hbm = pl.BlockSpec(memory_space=pltpu.HBM)
    return pl.pallas_call(
        functools.partial(gather_kernel, plan),
        out_shape=jax.ShapeDtypeStruct((groups, 2 * slots * WIN, plan.width), dtype),
        in_specs=[hbm, hbm, hbm, hbm],
        out_specs=pl.BlockSpec(memory_space=pltpu.VMEM),
        scratch_shapes=[
            pltpu.VMEM((streams, batch, channels, length), dtype),
            pltpu.VMEM((plan.rows, 2 * BINS, channels), jnp.float32),
            pltpu.VMEM((groups, plan.pieces, plan.rows, plan.width), dtype),
            pltpu.VMEM((groups, plan.pieces, 2, plan.half, plan.rows, plan.width), dtype),
            pltpu.VMEM((groups,) + source_map.shape, jnp.int32),
            pltpu.VMEM((groups, 2, 2 * slots * WIN, total // 2), dtype),
            pltpu.VMEM((1, 2, slots), jnp.int32),
            pltpu.VMEM(table.shape, dtype),
            pltpu.SemaphoreType.DMA((streams,)),
            pltpu.SemaphoreType.DMA((3,)),
            pltpu.SemaphoreType.DMA((groups, len(plan.parts), plan.half)),
            pltpu.SemaphoreType.DMA((groups, len(plan.parts))),
            pltpu.SemaphoreType.DMA((2, plan.half)),
            pltpu.SemaphoreType.DMA((groups, len(plan.parts))),
            pltpu.SemaphoreType.DMA((1,)),
            pltpu.SemaphoreType.DMA((groups,)),
            pltpu.SemaphoreType.DMA((groups,)),
            pltpu.SemaphoreType.DMA((groups,)),
            pltpu.SemaphoreType.DMA((plan.pieces,)),
        ],
        compiler_params=pltpu.CompilerParams(
            collective_id=0, has_side_effects=True, vmem_limit_bytes=48 << 20
        ),
        name="gather_picked",
    )(
        pltpu.with_memory_space_constraint(jnp.transpose(pair_blocks, (0, 2, 1)), pltpu.HBM),
        pltpu.with_memory_space_constraint(source_map, pltpu.HBM),
        pltpu.with_memory_space_constraint(table, pltpu.HBM),
        records,
    )


def stack_kernel(plan, scale, picked_ref, out_ref, done, sems):
    groups = plan.groups
    slots, bins, _, channels, _ = out_ref.shape

    def write(s, f):
        return pltpu.make_async_copy(done.at[s, f], out_ref.at[s, f], sems.at[s, f])

    for s in range(slots):
        left = slice(2 * s * WIN, (2 * s + 1) * WIN)
        right = slice((2 * s + 1) * WIN, (2 * s + 2) * WIN)
        for f in range(bins):
            real = slice(f * channels, (f + 1) * channels)
            imag = slice((bins + f) * channels, (bins + f + 1) * channels)
            x_re = [picked_ref[g, left, real] for g in range(groups)]
            x_im = [picked_ref[g, left, imag] for g in range(groups)]
            y_re = jnp.concatenate([picked_ref[g, right, real] for g in range(groups)], axis=0)
            y_im = jnp.concatenate([picked_ref[g, right, imag] for g in range(groups)], axis=0)
            lhs = jnp.concatenate(x_re + x_im, axis=0)
            rhs = jnp.concatenate(
                [
                    jnp.concatenate([y_re, -y_im], axis=1),
                    jnp.concatenate([y_im, y_re], axis=1),
                ],
                axis=0,
            )
            both = lax.dot_general(
                lhs, rhs, (((0,), (0,)), ((), ())), preferred_element_type=jnp.float32
            )
            done[s, f, 0] = both[:, :channels] * scale
            done[s, f, 1] = both[:, channels:] * scale
            write(s, f).start()
    for s in range(slots):
        for f in range(bins):
            write(s, f).wait()


def stack_pairs(plan, slots, picked):
    channels, bins = plan.channels, plan.bins
    scale = 1.0 / math.sqrt(WIN * plan.groups)
    vmem = pl.BlockSpec(memory_space=pltpu.VMEM)
    shape = (slots, bins, 2, channels, channels)
    return pl.pallas_call(
        functools.partial(stack_kernel, plan, scale),
        out_shape=jax.ShapeDtypeStruct(shape, jnp.float32),
        in_specs=[vmem],
        out_specs=pl.BlockSpec(memory_space=pl.ANY),
        scratch_shapes=[pltpu.VMEM(shape, jnp.float32), pltpu.SemaphoreType.DMA((slots, bins))],
        compiler_params=pltpu.CompilerParams(vmem_limit_bytes=40 << 20),
        name="stack_pairs",
    )(picked)


def per_device(groups, pairs, records, source_map, pair_blocks):
    table = jnp.asarray(transform_table(records.shape[3]))
    plan = Plan(groups, pairs, records.shape[1], records.shape[2])
    picked = gather_picked(plan, pair_blocks, source_map, table, records[0])
    return stack_pairs(plan, pair_blocks.shape[1], picked)


def solution(mesh):
    groups, pairs = mesh.shape["tm"], mesh.shape["pairs"]
    return jax.shard_map(
        functools.partial(per_device, groups, pairs),
        mesh=mesh,
        in_specs=(P("tm", "pairs", None, None), P("tm", None), P("pairs", None, None)),
        out_specs=P("pairs", "tm", None, None, None),
        check_vma=False,
    )
```
